128 devices in a mesh: freq: 16 (over x, z_lo, core), src: 8 (over y, z_hi).
Axes of the slice: x: 4, y: 4, z: 4 (z_hi: 2, z_lo: 2; z = z_hi * 2 + z_lo), core: 2. Of those that a mesh axis runs over, the one named last changes fastest.
Arguments:
- focusing: bfloat16 [64, 1024, 2048], P('src', 'freq'), may hold values from -6 to 6
- direct: bfloat16 [64, 1024, 2048], P('src', 'freq'), may hold values from -6 to 6
- kernel: bfloat16 [2, 192, 2048, 1024], P(None, 'freq', 'src'), may hold values from -0.125 to 0.125
- onset_up: int32 [64, 2048], P('freq', 'src'), may hold values from 256 to 2048
- onset_back: int32 [64, 1024], P('src', 'freq'), may hold values from 256 to 2048
Outputs:
- upgoing: bfloat16 [64, 2048, 2048], P('freq', 'src')
- updated: bfloat16 [64, 1024, 2048], P('src', 'freq')
The draws below stay inside these ranges and needn't reach their ends.
All inputs are finite; a program needn't handle non-finite values.
Results may differ from the reference program's by a relative error of at most 0.008.
Values may be sent and summed in bfloat16 or wider, within the bound.
No kernel may reach another device: no remote copies, remote signals or barrier semaphores. Data moves between devices by JAX's collectives and lax.ppermute only.
A program may use at most 128 MiB of HBM per device.

```python
import math
import jax
import jax.numpy as jnp
from jax import lax

NT = 2048
NF = 192
BIN0 = 16
S = 2048
R = 1024
P_SIZE = 64
N_SRC = 8


def with_ends(result, rng, least, largest):
    dims = result.shape
    spot = [jax.random.randint(jax.random.fold_in(rng, axis), (), 0, dims[axis]) for axis in range(len(dims))]
    result = result.at[tuple(spot)].set(least)
    longest = dims.index(max(dims))
    spot[longest] = (spot[longest] + 1) % dims[longest]
    return result.at[tuple(spot)].set(largest)


def shard_levels(key, dims, split, least, top_value):
    gain, own = 1.0, jax.random.fold_in(key, 6)
    for dim, parts in split:
        steps = jnp.exp(jax.random.uniform(jax.random.fold_in(own, dim), (parts,), jnp.float32, least / len(split), top_value / len(split)))
        gain = gain * jnp.repeat(steps, dims[dim] // parts).reshape([-1 if axis == dim else 1 for axis in range(len(dims))])
    return gain


def gaussian(key, shape, width, limit, split=(), kind=jnp.bfloat16):
    entries = width * jax.random.normal(key, shape, jnp.float32)
    if split:
        entries = entries * shard_levels(key, shape, split, -0.22, 0.18)
    return jnp.clip(entries, -limit, limit).astype(kind)


def setup_inputs(seed: int = 0) -> dict:
    key_list = jax.random.split(jax.random.key(seed), 6)
    return {
        "focusing": gaussian(key_list[0], (P_SIZE, R, NT), 1.0, 6.0, ((0, 8), (1, 16))),
        "direct": gaussian(key_list[1], (P_SIZE, R, NT), 1.0, 6.0, ((0, 8), (1, 16))),
        "kernel": gaussian(key_list[2], (2, NF, S, R), (2 * R) ** -0.5, 0.125, ((1, 16), (2, 8))),
        "onset_up": with_ends(jax.random.randint(key_list[3], (P_SIZE, S), NT // 8, NT + 1), jax.random.fold_in(key_list[3], 1), NT // 8, NT).astype(jnp.int32),
        "onset_back": with_ends(jax.random.randint(key_list[4], (P_SIZE, R), NT // 8, NT + 1), jax.random.fold_in(key_list[4], 1), NT // 8, NT).astype(jnp.int32),
    }


def frequency_band_tables():
    sample_index = jnp.arange(NT, dtype=jnp.int32)
    bin_index = BIN0 + jnp.arange(NF, dtype=jnp.int32)
    phase = (sample_index[:, None] * bin_index[None, :]) % NT
    angle = phase.astype(jnp.float32) * (2.0 * math.pi / NT)
    cosine = jnp.cos(angle)
    sine = jnp.sin(angle)
    forward_table = jnp.stack([cosine, -sine], axis=2).reshape(NT, 2 * NF).astype(jnp.bfloat16)
    inverse_table = ((2.0 / NT) * jnp.stack([cosine.T, -sine.T], axis=1)).reshape(2 * NF, NT).astype(jnp.bfloat16)
    return forward_table, inverse_table


def reference(focusing, direct, kernel, onset_up, onset_back):
    forward_table, inverse_table = frequency_band_tables()
    highest = lax.Precision.HIGHEST
    spectrum = jnp.dot(focusing.reshape(P_SIZE * R, NT), forward_table, preferred_element_type=jnp.float32)
    spectrum = spectrum.astype(jnp.bfloat16).reshape(P_SIZE, R, NF, 2)
    sample_index = jnp.arange(NT, dtype=jnp.int32)

    def forward_one(index):
        kernel_real_part = kernel[0, index].astype(jnp.float32)
        kernel_imaginary = kernel[1, index].astype(jnp.float32)
        spectral_real = spectrum[:, :, index, 0].astype(jnp.float32)
        spectral_imaginary = spectrum[:, :, index, 1].astype(jnp.float32)
        wave_real = jnp.dot(spectral_real, kernel_real_part.T, precision=highest) - jnp.dot(spectral_imaginary, kernel_imaginary.T, precision=highest)
        wave_imag = jnp.dot(spectral_imaginary, kernel_real_part.T, precision=highest) + jnp.dot(spectral_real, kernel_imaginary.T, precision=highest)
        return jnp.stack([wave_real, wave_imag]).astype(jnp.bfloat16)

    waves = lax.map(forward_one, jnp.arange(NF, dtype=jnp.int32))

    def time_one(point):
        block = waves[:, :, point, :].reshape(2 * NF, S)
        signal = jnp.dot(block.T, inverse_table, preferred_element_type=jnp.float32)
        kept = jnp.where(sample_index[None, :] < onset_up[point][:, None], signal, 0.0).astype(jnp.bfloat16)
        back = jnp.dot(kept, forward_table, preferred_element_type=jnp.float32).astype(jnp.bfloat16)
        return kept, back

    upgoing, back_spectrum = lax.map(time_one, jnp.arange(P_SIZE, dtype=jnp.int32))
    back_spectrum = back_spectrum.reshape(P_SIZE, S, NF, 2)

    def adjoint_one(index):
        blocks = S // N_SRC
        backward_real = back_spectrum[:, :, index, 0].astype(jnp.float32).reshape(P_SIZE, N_SRC, blocks)
        backward_imaginary = back_spectrum[:, :, index, 1].astype(jnp.float32).reshape(P_SIZE, N_SRC, blocks)
        kernel_real_part = kernel[0, index].astype(jnp.float32).reshape(N_SRC, blocks, R)
        kernel_imaginary = kernel[1, index].astype(jnp.float32).reshape(N_SRC, blocks, R)
        term_real = jnp.einsum("pbs,bsr->bpr", backward_real, kernel_real_part, precision=highest) + jnp.einsum("pbs,bsr->bpr", backward_imaginary, kernel_imaginary, precision=highest)
        term_imag = jnp.einsum("pbs,bsr->bpr", backward_imaginary, kernel_real_part, precision=highest) - jnp.einsum("pbs,bsr->bpr", backward_real, kernel_imaginary, precision=highest)
        sum_real = lax.optimization_barrier(term_real.astype(jnp.bfloat16)).astype(jnp.float32).sum(0)
        sum_imag = lax.optimization_barrier(term_imag.astype(jnp.bfloat16)).astype(jnp.float32).sum(0)
        return jnp.stack([sum_real, sum_imag]).astype(jnp.bfloat16)

    adjoint = lax.map(adjoint_one, jnp.arange(NF, dtype=jnp.int32))

    def trace_one(point):
        block = adjoint[:, :, point, :].reshape(2 * NF, R)
        trace = jnp.dot(block.T, inverse_table, preferred_element_type=jnp.float32)
        cut = jnp.where(sample_index[None, :] < onset_back[point][:, None], trace, 0.0)
        return (direct[point].astype(jnp.float32) - cut).astype(jnp.bfloat16)

    updated = lax.map(trace_one, jnp.arange(P_SIZE, dtype=jnp.int32))
    return upgoing, updated
```

```python
import functools
import math

import jax
import jax.numpy as jnp
from jax import lax
from jax.experimental import pallas as pl
from jax.experimental.pallas import tpu as pltpu
from jax.sharding import PartitionSpec as P

NT = 2048
NF = 192
BIN0 = 16
NFREQ = 16
NSRC = 8
NY = 4
J = NF // NFREQ
ROWS = 2 * NF
BLOCK = 2 * J
POINTS = 8
UP_POINTS = 4
RECV = 64
R = NFREQ * RECV
SOURCES = 256
SCALE = 2.0 / NT
F32 = jnp.float32
BF16 = jnp.bfloat16


NT_DIMS = (((1,), (1,)), ((), ()))
TN_DIMS = (((0,), (0,)), ((), ()))

RELATIVE = ((0, 0), (3, 0), (1, 0), (2, 0), (0, 1), (3, 1), (1, 1), (2, 1))


def params(limit=60):
    return pltpu.CompilerParams(
        dimension_semantics=("arbitrary",), vmem_limit_bytes=limit << 20
    )


def cost(flops, bytes_accessed):
    return pl.CostEstimate(flops=flops, bytes_accessed=bytes_accessed, transcendentals=0)


def write_table(table):
    lane = lax.broadcasted_iota(jnp.int32, (ROWS, 128), 1)
    row = lax.broadcasted_iota(jnp.int32, (ROWS, 128), 0)
    bin_index = BIN0 + row // 2
    quarter = row % 2
    step = 2.0 * math.pi / NT
    fine = (lane * bin_index % NT).astype(F32) * step
    coarse = ((lane * bin_index + 4 * quarter) % 16).astype(F32) * (2.0 * math.pi / 16)
    fine_cos, fine_sin = jnp.cos(fine), jnp.sin(fine)
    coarse_cos, coarse_sin = jnp.cos(coarse), jnp.sin(coarse)
    for a in range(NT // 128):
        value = coarse_cos[:, a : a + 1] * fine_cos - coarse_sin[:, a : a + 1] * fine_sin
        table[:, a * 128 : (a + 1) * 128] = value.astype(BF16)


def spectrum_body(traces, table, out):
    @pl.when(pl.program_id(0) == 0)
    def _():
        write_table(table)

    out[...] = lax.dot_general(
        table[...], traces[...], NT_DIMS, preferred_element_type=F32
    ).astype(BF16)


def spectrum(traces):
    count = traces.shape[0]
    tile = 128
    return pl.pallas_call(
        spectrum_body,
        grid=(count // tile,),
        in_specs=[pl.BlockSpec((tile, NT), lambda i: (i, 0))],
        out_specs=[
            pl.BlockSpec((ROWS, NT), lambda i: (0, 0)),
            pl.BlockSpec((ROWS, tile), lambda i: (0, i)),
        ],
        out_shape=[
            jax.ShapeDtypeStruct((ROWS, NT), BF16),
            jax.ShapeDtypeStruct((ROWS, count), BF16),
        ],
        compiler_params=params(),
        cost_estimate=cost(2 * count * NT * ROWS, 4 << 20),
        name="spectrum",
    )(traces)


def forward_body(place, *refs):
    blocks, kern, out = refs[:NSRC], refs[NSRC], refs[NSRC + 1]
    field = jnp.concatenate([b[0] for b in blocks], axis=0)
    by_real = lax.dot_general(field, kern[0, 0], NT_DIMS, preferred_element_type=F32)
    by_imag = lax.dot_general(field, kern[1, 0], NT_DIMS, preferred_element_type=F32)
    for rel in range(NSRC):
        r0 = rel * 2 * POINTS
        r1 = r0 + POINTS
        real = by_real[r0:r1] - by_imag[r1 : r1 + POINTS]
        imag = by_real[r1 : r1 + POINTS] + by_imag[r0:r1]
        out[place[rel], 0] = jnp.concatenate([real, imag], axis=0).astype(BF16)


def forward(place, blocks, kern):
    return pl.pallas_call(
        forward_body,
        grid_spec=pltpu.PrefetchScalarGridSpec(
            num_scalar_prefetch=1,
            grid=(J,),
            in_specs=[pl.BlockSpec((1, 2 * POINTS, R), lambda j, p: (j, 0, 0))] * NSRC
            + [pl.BlockSpec((2, 1, SOURCES, R), lambda j, p: (0, j, 0, 0))],
            out_specs=pl.BlockSpec((NSRC, 1, 2 * POINTS, SOURCES), lambda j, p: (0, j, 0, 0)),
        ),
        out_shape=jax.ShapeDtypeStruct((NSRC, J, 2 * POINTS, SOURCES), BF16),
        compiler_params=params(),
        cost_estimate=cost(8 * J * 64 * SOURCES * R, 16 << 20),
        name="forward",
    )(place, *blocks, kern)


def adjoint_body(place, field_ref, kern, *outs):
    field = jnp.concatenate([field_ref[0, place[rel]] for rel in range(NSRC)], axis=0)
    by_real = jnp.dot(field, kern[0, 0], preferred_element_type=F32)
    by_imag = jnp.dot(field, kern[1, 0], preferred_element_type=F32)
    for rel in range(NSRC):
        r0 = rel * 2 * POINTS
        r1 = r0 + POINTS
        real = by_real[r0:r1] + by_imag[r1 : r1 + POINTS]
        imag = by_real[r1 : r1 + POINTS] - by_imag[r0:r1]
        outs[rel][0] = jnp.concatenate([real, imag], axis=0).astype(BF16)


def adjoint(place, field, kern):
    return pl.pallas_call(
        adjoint_body,
        grid_spec=pltpu.PrefetchScalarGridSpec(
            num_scalar_prefetch=1,
            grid=(J,),
            in_specs=[
                pl.BlockSpec((1, NSRC, 2 * POINTS, SOURCES), lambda j, p: (j, 0, 0, 0)),
                pl.BlockSpec((2, 1, SOURCES, R), lambda j, p: (0, j, 0, 0)),
            ],
            out_specs=[pl.BlockSpec((1, 2 * POINTS, R), lambda j, p: (j, 0, 0))] * NSRC,
        ),
        out_shape=[jax.ShapeDtypeStruct((J, 2 * POINTS, R), BF16)] * NSRC,
        compiler_params=params(),
        cost_estimate=cost(8 * J * 64 * SOURCES * R, 16 << 20),
        name="adjoint",
    )(place, field, kern)


def truncate_body(waves, table, onset, up, back):
    signal = lax.dot_general(waves[...], table[...], TN_DIMS, preferred_element_type=F32) * SCALE
    sample = lax.broadcasted_iota(jnp.int32, signal.shape, 1)
    kept = jnp.where(sample < onset[...], signal, 0.0).astype(BF16)
    up[...] = kept
    back[...] = lax.dot_general(
        table[...], kept, NT_DIMS, preferred_element_type=F32
    ).astype(BF16)


def truncate(waves, table, onset):
    count = waves.shape[1]
    tile = SOURCES
    return pl.pallas_call(
        truncate_body,
        grid=(count // tile,),
        in_specs=[
            pl.BlockSpec((ROWS, tile), lambda i: (0, i)),
            pl.BlockSpec((ROWS, NT), lambda i: (0, 0)),
            pl.BlockSpec((tile, 1), lambda i: (i, 0)),
        ],
        out_specs=[
            pl.BlockSpec((tile, NT), lambda i: (i, 0)),
            pl.BlockSpec((ROWS, tile), lambda i: (0, i)),
        ],
        out_shape=[
            jax.ShapeDtypeStruct((count, NT), BF16),
            jax.ShapeDtypeStruct((ROWS, count), BF16),
        ],
        compiler_params=params(),
        cost_estimate=cost(4 * count * NT * ROWS, 8 << 20),
        name="truncate",
    )(waves, table, onset)


def update_body(bins, table, direct, onset, out):
    trace = lax.dot_general(bins[...], table[...], TN_DIMS, preferred_element_type=F32) * SCALE
    sample = lax.broadcasted_iota(jnp.int32, trace.shape, 1)
    cut = jnp.where(sample < onset[...], trace, 0.0)
    out[...] = (direct[...].astype(F32) - cut).astype(BF16)


def update(bins, table, direct, onset):
    count = bins.shape[1]
    tile = 128
    return pl.pallas_call(
        update_body,
        grid=(count // tile,),
        in_specs=[
            pl.BlockSpec((ROWS, tile), lambda i: (0, i)),
            pl.BlockSpec((ROWS, NT), lambda i: (0, 0)),
            pl.BlockSpec((tile, NT), lambda i: (i, 0)),
            pl.BlockSpec((tile, 1), lambda i: (i, 0)),
        ],
        out_specs=pl.BlockSpec((tile, NT), lambda i: (i, 0)),
        out_shape=jax.ShapeDtypeStruct((count, NT), BF16),
        compiler_params=params(),
        cost_estimate=cost(2 * count * NT * ROWS, 6 << 20),
        name="update",
    )(bins, table, direct, onset)


def shift(value, dy, dz):
    pairs = [
        (2 * y + z, 2 * ((y + dy) % NY) + (z + dz) % 2) for y in range(NY) for z in range(2)
    ]
    return lax.ppermute(value, "src", pairs)


def gather_blocks(own):
    across = shift(own, 0, 1)
    up = shift(own, 1, 0)
    down = shift(own, -1, 0)
    across_up = shift(across, 1, 0)
    across_down = shift(across, -1, 0)
    far = shift(up, 1, 0)
    across_far = shift(across_down, -1, 0)
    return [own, up, down, far, across, across_up, across_down, across_far]


def add(*terms):
    return functools.reduce(lambda a, b: a + b, [t.astype(F32) for t in terms]).astype(BF16)


def reduce_blocks(terms):
    own, up, down, far, across, across_up, across_down, across_far = terms
    r1 = shift(across_far, 1, 0)
    r5 = shift(far, -1, 0)
    r3 = shift(across_up, -1, 0)
    r2 = shift(add(across_down, r1), 1, 0)
    r6 = shift(add(up, r5), -1, 0)
    r4 = shift(add(across, r2, r3), 0, 1)
    r7 = shift(down, 1, 0)
    return add(own, r6, r7, r4)


def exchange(value):
    return lax.all_to_all(value, "freq", split_axis=0, concat_axis=0, tiled=True)


def local(focusing, direct, kernel, onset_up, onset_back):
    me = lax.axis_index("src")
    my_y, my_z = me // 2, me % 2
    place = jnp.stack([2 * ((my_y + dy) % NY) + (my_z + dz) % 2 for dy, dz in RELATIVE])

    table, bins = spectrum(focusing.reshape(POINTS * RECV, NT))
    bins = exchange(bins.reshape(NFREQ, BLOCK, POINTS * RECV))
    own = bins.reshape(NFREQ, J, 2, POINTS, RECV).transpose(1, 2, 3, 0, 4)
    blocks = gather_blocks(own.reshape(J, 2 * POINTS, R))

    waves = forward(place, blocks, kernel)
    waves = waves.reshape(NSRC, J, 2, 2, UP_POINTS, SOURCES).transpose(0, 3, 1, 2, 4, 5)
    waves = exchange(waves.reshape(NFREQ, BLOCK, UP_POINTS * SOURCES))

    upgoing, back = truncate(
        waves.reshape(ROWS, UP_POINTS * SOURCES), table, onset_up.reshape(-1, 1)
    )
    back = exchange(back.reshape(NFREQ, BLOCK, UP_POINTS * SOURCES))
    back = back.reshape(NSRC, 2, J, 2, UP_POINTS, SOURCES).transpose(2, 0, 3, 1, 4, 5)

    terms = adjoint(place, back.reshape(J, NSRC, 2 * POINTS, SOURCES), kernel)
    summed = reduce_blocks(terms)
    summed = summed.reshape(J, 2, POINTS, NFREQ, RECV).transpose(3, 0, 1, 2, 4)
    summed = exchange(summed.reshape(NFREQ, BLOCK, POINTS * RECV))

    updated = update(
        summed.reshape(ROWS, POINTS * RECV),
        table,
        direct.reshape(POINTS * RECV, NT),
        onset_back.reshape(-1, 1),
    )
    return (
        upgoing.reshape(UP_POINTS, SOURCES, NT),
        updated.reshape(POINTS, RECV, NT),
    )


def solution(mesh):
    placed = (
        P("src", "freq", None),
        P("src", "freq", None),
        P(None, "freq", "src", None),
        P("freq", "src"),
        P("src", "freq"),
    )
    return jax.shard_map(
        local,
        mesh=mesh,
        in_specs=placed,
        out_specs=(P("freq", "src", None), P("src", "freq", None)),
        check_vma=False,
    )
```

```python
import functools
import math

import jax
import jax.numpy as jnp
from jax import lax
from jax.experimental import pallas as pl
from jax.experimental.pallas import tpu as pltpu
from jax.sharding import PartitionSpec as P

NT = 2048
NF = 192
BIN0 = 16
NFREQ = 16
NSRC = 8
NY = 4
J = NF // NFREQ
ROWS = 2 * NF
BLOCK = 2 * J
POINTS = 8
UP_POINTS = 4
RECV = 64
R = NFREQ * RECV
SOURCES = 256
SCALE = 2.0 / NT
F32 = jnp.float32
BF16 = jnp.bfloat16


NT_DIMS = (((1,), (1,)), ((), ()))
TN_DIMS = (((0,), (0,)), ((), ()))

RELATIVE = ((0, 0), (3, 0), (1, 0), (2, 0), (0, 1), (3, 1), (1, 1), (2, 1))


LIMIT = 24 << 20
VMEM_SPEC = pl.BlockSpec(memory_space=pltpu.VMEM)
SMEM_SPEC = pl.BlockSpec(memory_space=pltpu.SMEM)
HBM_SPEC = pl.BlockSpec(memory_space=pltpu.HBM)


def params(limit=24):
    return pltpu.CompilerParams(
        dimension_semantics=("arbitrary",), vmem_limit_bytes=limit << 20
    )


def cost(flops, bytes_accessed):
    return pl.CostEstimate(flops=flops, bytes_accessed=bytes_accessed, transcendentals=0)


def write_table(table):
    lane = lax.broadcasted_iota(jnp.int32, (ROWS, 128), 1)
    row = lax.broadcasted_iota(jnp.int32, (ROWS, 128), 0)
    bin_index = BIN0 + row // 2
    quarter = row % 2
    step = 2.0 * math.pi / NT
    fine = (lane * bin_index % NT).astype(F32) * step
    coarse = ((lane * bin_index + 4 * quarter) % 16).astype(F32) * (2.0 * math.pi / 16)
    fine_cos, fine_sin = jnp.cos(fine), jnp.sin(fine)
    coarse_cos, coarse_sin = jnp.cos(coarse), jnp.sin(coarse)
    for a in range(NT // 128):
        value = coarse_cos[:, a : a + 1] * fine_cos - coarse_sin[:, a : a + 1] * fine_sin
        table[:, a * 128 : (a + 1) * 128] = value.astype(BF16)


def spectrum_body(traces, table, out):
    @pl.when(pl.program_id(0) == 0)
    def _():
        write_table(table)

    out[...] = lax.dot_general(
        table[...], traces[...], NT_DIMS, preferred_element_type=F32
    ).astype(BF16)


def spectrum(traces):
    count = traces.shape[0]
    tile = 128
    return pl.pallas_call(
        spectrum_body,
        grid=(count // tile,),
        in_specs=[pl.BlockSpec((tile, NT), lambda i: (i, 0))],
        out_specs=[
            pl.BlockSpec((ROWS, NT), lambda i: (0, 0)),
            pl.BlockSpec((ROWS, tile), lambda i: (0, i)),
        ],
        out_shape=[
            jax.ShapeDtypeStruct((ROWS, NT), BF16),
            jax.ShapeDtypeStruct((ROWS, count), BF16),
        ],
        compiler_params=params(),
        cost_estimate=cost(2 * count * NT * ROWS, 4 << 20),
        name="spectrum",
    )(traces)


def swapped(value, sign):
    rows, lanes = value.shape
    tiles = value.reshape(rows // 8, 2, 4, lanes)
    return jnp.concatenate([-sign * tiles[:, 1:], sign * tiles[:, :1]], axis=1).reshape(rows, lanes)


def places(me):
    y, z = me // 2, me % 2
    return [2 * ((y + dy) % NY) + (z + dz) % 2 for dy, dz in RELATIVE]


def hold_body(kern, held, sems):
    copies = [
        pltpu.make_async_copy(kern.at[part], held.at[part], sems.at[part]) for part in range(2)
    ]
    for copy in copies:
        copy.start()
    for copy in copies:
        copy.wait()


def hold(kern):
    return pl.pallas_call(
        hold_body,
        in_specs=[HBM_SPEC],
        out_specs=pl.BlockSpec(memory_space=pl.ANY),
        out_shape=pltpu.VMEM(kern.shape, BF16),
        scratch_shapes=[pltpu.SemaphoreType.DMA((2,))],
        compiler_params=pltpu.CompilerParams(vmem_limit_bytes=1 << 20),
        cost_estimate=cost(0, 13 << 20),
        name="hold",
    )(kern)


def forward_body(me, *refs):
    blocks, kern, out = refs[:NSRC], refs[NSRC], refs[NSRC + 1]
    place = places(me[0])

    def step(j, carry):
        field = jnp.concatenate([b[j] for b in blocks], axis=0)
        by_real = lax.dot_general(field, kern[0, j], NT_DIMS, preferred_element_type=F32)
        by_imag = lax.dot_general(field, kern[1, j], NT_DIMS, preferred_element_type=F32)
        waves = (by_real + swapped(by_imag, 1.0)).astype(BF16).reshape(NSRC, 2, 8, SOURCES)
        for rel in range(NSRC):
            for half in range(2):
                out[2 * place[rel] + half, j] = waves[rel, half]
        return carry

    lax.fori_loop(0, J, step, 0)


def forward(me, blocks, kern):
    return pl.pallas_call(
        forward_body,
        in_specs=[SMEM_SPEC] + [VMEM_SPEC] * (NSRC + 1),
        out_specs=VMEM_SPEC,
        out_shape=jax.ShapeDtypeStruct((NFREQ, J, 8, SOURCES), BF16),
        compiler_params=pltpu.CompilerParams(vmem_limit_bytes=LIMIT),
        cost_estimate=cost(8 * J * 64 * SOURCES * R, 4 << 20),
        name="forward",
    )(me, *blocks, kern)


def adjoint_body(me, field_ref, kern, *refs):
    outs, held, sems = refs[:NSRC], refs[NSRC], refs[NSRC + 1]
    place = places(me[0])

    def copies(j):
        return [
            pltpu.make_async_copy(kern.at[part, j], held.at[part, j], sems.at[part, j])
            for part in range(2)
        ]

    for j in range(J):
        for copy in copies(j):
            copy.start()

    def step(j, carry):
        field = jnp.concatenate(
            [field_ref[2 * place[rel] + half, j] for rel in range(NSRC) for half in range(2)], axis=0
        )
        for copy in copies(j):
            copy.wait()
        by_real = jnp.dot(field, held[0, j], preferred_element_type=F32)
        by_imag = jnp.dot(field, held[1, j], preferred_element_type=F32)
        terms = (by_real + swapped(by_imag, -1.0)).astype(BF16)
        for rel in range(NSRC):
            outs[rel][j] = terms[rel * 16 : rel * 16 + 16]
        return carry

    lax.fori_loop(0, J, step, 0)


def adjoint(me, field, kern):
    return pl.pallas_call(
        adjoint_body,
        in_specs=[SMEM_SPEC, VMEM_SPEC, HBM_SPEC],
        out_specs=[VMEM_SPEC] * NSRC,
        out_shape=[jax.ShapeDtypeStruct((J, 2 * POINTS, R), BF16)] * NSRC,
        scratch_shapes=[pltpu.VMEM(kern.shape, BF16), pltpu.SemaphoreType.DMA((2, J))],
        compiler_params=pltpu.CompilerParams(vmem_limit_bytes=LIMIT),
        cost_estimate=cost(8 * J * 64 * SOURCES * R, 16 << 20),
        name="adjoint",
    )(me, field, kern)


def truncate_body(waves, table, onset, up, back, wide_in, wide_out):
    step = pl.program_id(0)
    last = pl.num_programs(0) - 1

    @pl.when(step == 0)
    def _():
        for half in range(SOURCES // 128):
            wide_in[half] = waves[:, half * 128 : half * 128 + 128].astype(F32)

    every = pl.ds(step, ROWS, stride=UP_POINTS)
    mine = jnp.concatenate(
        [wide_in.at[half][every, :] for half in range(SOURCES // 128)], axis=1
    ).astype(BF16)
    signal = lax.dot_general(mine, table[...], TN_DIMS, preferred_element_type=F32) * SCALE
    sample = lax.broadcasted_iota(jnp.int32, signal.shape, 1)
    kept = jnp.where(sample < onset[...], signal, 0.0).astype(BF16)
    up[...] = kept
    bins = lax.dot_general(table[...], kept, NT_DIMS, preferred_element_type=F32)
    for half in range(SOURCES // 128):
        wide_out.at[half][every, :] = bins[:, half * 128 : half * 128 + 128]

    @pl.when(step == last)
    def _():
        for half in range(SOURCES // 128):
            back[:, half * 128 : half * 128 + 128] = wide_out[half].astype(BF16)


def truncate(waves, table, onset):
    rows = waves.shape[0]
    return pl.pallas_call(
        truncate_body,
        grid=(UP_POINTS,),
        in_specs=[
            pl.BlockSpec((rows, SOURCES), lambda i: (0, 0)),
            pl.BlockSpec((ROWS, NT), lambda i: (0, 0)),
            pl.BlockSpec((SOURCES, 1), lambda i: (i, 0)),
        ],
        out_specs=[
            pl.BlockSpec((SOURCES, NT), lambda i: (i, 0)),
            pl.BlockSpec((rows, SOURCES), lambda i: (0, 0)),
        ],
        out_shape=[
            jax.ShapeDtypeStruct((UP_POINTS * SOURCES, NT), BF16),
            jax.ShapeDtypeStruct((rows, SOURCES), BF16),
        ],
        scratch_shapes=[pltpu.VMEM((SOURCES // 128, rows, 128), F32)] * 2,
        compiler_params=params(),
        cost_estimate=cost(4 * UP_POINTS * SOURCES * NT * ROWS, 8 << 20),
        name="truncate",
    )(waves, table, onset)


def update_body(bins, table, direct, onset, out):
    trace = lax.dot_general(bins[...], table[...], TN_DIMS, preferred_element_type=F32) * SCALE
    sample = lax.broadcasted_iota(jnp.int32, trace.shape, 1)
    cut = jnp.where(sample < onset[...], trace, 0.0)
    out[...] = (direct[...].astype(F32) - cut).astype(BF16)


def update(bins, table, direct, onset):
    count = bins.shape[1]
    tile = 128
    return pl.pallas_call(
        update_body,
        grid=(count // tile,),
        in_specs=[
            pl.BlockSpec((ROWS, tile), lambda i: (0, i)),
            pl.BlockSpec((ROWS, NT), lambda i: (0, 0)),
            pl.BlockSpec((tile, NT), lambda i: (i, 0)),
            pl.BlockSpec((tile, 1), lambda i: (i, 0)),
        ],
        out_specs=pl.BlockSpec((tile, NT), lambda i: (i, 0)),
        out_shape=jax.ShapeDtypeStruct((count, NT), BF16),
        compiler_params=params(),
        cost_estimate=cost(2 * count * NT * ROWS, 6 << 20),
        name="update",
    )(bins, table, direct, onset)


def shift(value, dy, dz):
    pairs = [
        (2 * y + z, 2 * ((y + dy) % NY) + (z + dz) % 2) for y in range(NY) for z in range(2)
    ]
    return lax.ppermute(value, "src", pairs)


def gather_blocks(own):
    across = shift(own, 0, 1)
    up = shift(own, 1, 0)
    down = shift(own, -1, 0)
    across_up = shift(across, 1, 0)
    across_down = shift(across, -1, 0)
    far = shift(up, 1, 0)
    across_far = shift(across_down, -1, 0)
    return [own, up, down, far, across, across_up, across_down, across_far]


def add(*terms):
    return functools.reduce(lambda a, b: a + b, [t.astype(F32) for t in terms]).astype(BF16)


def reduce_blocks(terms):
    own, up, down, far, across, across_up, across_down, across_far = terms
    r1 = shift(across_far, 1, 0)
    r5 = shift(far, -1, 0)
    r3 = shift(across_up, -1, 0)
    r2 = shift(add(across_down, r1), 1, 0)
    r6 = shift(add(up, r5), -1, 0)
    r4 = shift(add(across, r2, r3), 0, 1)
    r7 = shift(down, 1, 0)
    return add(own, r6, r7, r4)


def exchange(value):
    return lax.all_to_all(value, "freq", split_axis=0, concat_axis=0, tiled=True)


def local(focusing, direct, kernel, onset_up, onset_back):
    me = lax.axis_index("src").reshape(1)
    up_onset = onset_up.reshape(-1, 1)
    back_onset = onset_back.reshape(-1, 1)

    table, bins = spectrum(
        pltpu.with_memory_space_constraint(focusing.reshape(POINTS * RECV, NT), pltpu.HBM)
    )
    bins, me, up_onset, back_onset = lax.optimization_barrier((bins, me, up_onset, back_onset))
    bins = exchange(bins.reshape(NFREQ, BLOCK, POINTS * RECV))
    own = bins.reshape(NFREQ, J, 2, 2, UP_POINTS, RECV).transpose(1, 3, 2, 4, 0, 5)
    own = own.reshape(J, 2 * POINTS, R)
    own, late_kernel = lax.optimization_barrier((own, kernel))
    late_kernel = pltpu.with_memory_space_constraint(late_kernel, pltpu.HBM)
    blocks = gather_blocks(own)

    waves = exchange(forward(me, blocks, hold(late_kernel)))

    upgoing, back = truncate(
        waves.reshape(NFREQ * J * 8, SOURCES), table, up_onset
    )
    back = exchange(back.reshape(NFREQ, J, 8, SOURCES))

    terms = adjoint(me, back, pltpu.with_memory_space_constraint(kernel, pltpu.HBM))
    summed = reduce_blocks(terms)
    summed = summed.reshape(J, 2, 2, UP_POINTS, NFREQ, RECV).transpose(4, 0, 2, 1, 3, 5)
    summed = exchange(summed.reshape(NFREQ, BLOCK, POINTS * RECV))

    updated = update(
        summed.reshape(ROWS, POINTS * RECV),
        table,
        direct.reshape(POINTS * RECV, NT),
        back_onset,
    )
    return (
        upgoing.reshape(UP_POINTS, SOURCES, NT),
        updated.reshape(POINTS, RECV, NT),
    )


def solution(mesh):
    placed = (
        P("src", "freq", None),
        P("src", "freq", None),
        P(None, "freq", "src", None),
        P("freq", "src"),
        P("src", "freq"),
    )
    return jax.shard_map(
        local,
        mesh=mesh,
        in_specs=placed,
        out_specs=(P("freq", "src", None), P("src", "freq", None)),
        check_vma=False,
    )
```

```python
import functools
import math

import jax
import jax.numpy as jnp
from jax import lax
from jax.experimental import pallas as pl
from jax.experimental.pallas import tpu as pltpu
from jax.sharding import PartitionSpec as P


NT = 2048
NF = 192
BIN0 = 16
NFREQ = 16
NY = 4
J = NF // NFREQ
ROWS = 2 * NF
BLOCK = 2 * J
POINTS = 8
UP_POINTS = 4
RECV = 64
R = NFREQ * RECV
SOURCES = 256
SCALE = 2.0 / NT
F32 = jnp.float32
BF16 = jnp.bfloat16


NT_DIMS = (((1,), (1,)), ((), ()))
TN_DIMS = (((0,), (0,)), ((), ()))

OWN, UP, DOWN, FAR, ACROSS, ACROSS_UP, ACROSS_DOWN, ACROSS_FAR = range(8)
RELATIVE = ((0, 0), (3, 0), (1, 0), (2, 0), (0, 1), (3, 1), (1, 1), (2, 1))
NEAR = (OWN, UP, DOWN, ACROSS)
REMOTE = (FAR, ACROSS_UP, ACROSS_DOWN, ACROSS_FAR)


VMEM_SPEC = pl.BlockSpec(memory_space=pltpu.VMEM)
SMEM_SPEC = pl.BlockSpec(memory_space=pltpu.SMEM)
HBM_SPEC = pl.BlockSpec(memory_space=pltpu.HBM)


def params(limit=24):
    return pltpu.CompilerParams(
        dimension_semantics=("arbitrary",), vmem_limit_bytes=limit << 20
    )


def cost(flops, bytes_accessed):
    return pl.CostEstimate(flops=flops, bytes_accessed=bytes_accessed, transcendentals=0)


def turn(phase):
    quarter = (phase + NT // 8) >> 9
    rest = (phase - (quarter << 9)).astype(F32) * (2.0 * math.pi / NT)
    square = rest * rest
    sine = rest * (
        1.0 + square * (-1.0 / 6 + square * (1.0 / 120 + square * (-1.0 / 5040 + square / 362880)))
    )
    cosine = 1.0 + square * (
        -0.5 + square * (1.0 / 24 + square * (-1.0 / 720 + square * (1.0 / 40320 - square / 3628800)))
    )
    odd = (quarter & 1) == 1
    first, second = jnp.where(odd, sine, cosine), jnp.where(odd, cosine, sine)
    behind = ((quarter + 1) & 2) == 2
    below = (quarter & 2) == 2
    return jnp.where(behind, -first, first), jnp.where(below, -second, second)


def write_table(table):
    lane = lax.broadcasted_iota(jnp.int32, (ROWS, 128), 1)
    row = lax.broadcasted_iota(jnp.int32, (ROWS, 128), 0)
    bin_index = BIN0 + (row >> 1)
    quarter = row & 1
    fine_cos, fine_sin = turn((lane * bin_index) & (NT - 1))
    coarse_cos, coarse_sin = turn(((lane * bin_index + 4 * quarter) & 15) << 7)
    for a in range(NT // 128):
        value = coarse_cos[:, a : a + 1] * fine_cos - coarse_sin[:, a : a + 1] * fine_sin
        table[:, a * 128 : (a + 1) * 128] = value.astype(BF16)


def spectrum_body(traces, table, out):
    @pl.when(pl.program_id(0) == 0)
    def _():
        write_table(table)

    out[...] = lax.dot_general(
        table[...], traces[...], NT_DIMS, preferred_element_type=F32
    ).astype(BF16)


def spectrum(traces):
    count = traces.shape[0]
    tile = 128
    return pl.pallas_call(
        spectrum_body,
        grid=(count // tile,),
        in_specs=[pl.BlockSpec((tile, NT), lambda i: (i, 0))],
        out_specs=[
            pl.BlockSpec((ROWS, NT), lambda i: (0, 0)),
            pl.BlockSpec((ROWS, tile), lambda i: (0, i)),
        ],
        out_shape=[
            jax.ShapeDtypeStruct((ROWS, NT), BF16),
            jax.ShapeDtypeStruct((ROWS, count), BF16),
        ],
        compiler_params=params(),
        cost_estimate=cost(2 * count * NT * ROWS, 4 << 20),
        name="spectrum",
    )(traces)


def swapped(value, sign):
    rows, lanes = value.shape
    tiles = value.reshape(rows // 8, 2, 4, lanes)
    return jnp.concatenate([-sign * tiles[:, 1:], sign * tiles[:, :1]], axis=1).reshape(rows, lanes)


def places(me):
    y, z = me // 2, me % 2
    return [2 * ((y + dy) % NY) + (z + dz) % 2 for dy, dz in RELATIVE]


def hold_body(kern, held, sems):
    copies = [
        pltpu.make_async_copy(kern.at[part], held.at[part], sems.at[part]) for part in range(2)
    ]
    for copy in copies:
        copy.start()
    for copy in copies:
        copy.wait()


def hold(kern):
    return pl.pallas_call(
        hold_body,
        in_specs=[HBM_SPEC],
        out_specs=pl.BlockSpec(memory_space=pl.ANY),
        out_shape=pltpu.VMEM(kern.shape, BF16),
        scratch_shapes=[pltpu.SemaphoreType.DMA((2,))],
        compiler_params=pltpu.CompilerParams(vmem_limit_bytes=1 << 20),
        cost_estimate=cost(0, 13 << 20),
        name="hold",
    )(kern)


def waves_of(blocks, kern, j):
    field = jnp.concatenate([b[j] for b in blocks], axis=0)
    by_real = lax.dot_general(field, kern[0, j], NT_DIMS, preferred_element_type=F32)
    by_imag = lax.dot_general(field, kern[1, j], NT_DIMS, preferred_element_type=F32)
    waves = (by_real + swapped(by_imag, 1.0)).astype(BF16)
    return waves.reshape(len(blocks), 2, 8, SOURCES)


def forward_near_body(*refs):
    *blocks, kern, out = refs

    def step(j, carry):
        waves = waves_of(blocks, kern, j)
        for index in range(len(blocks)):
            for half in range(2):
                out[2 * index + half, j] = waves[index, half]
        return carry

    lax.fori_loop(0, J, step, 0)


def forward_near(blocks, kern):
    return pl.pallas_call(
        forward_near_body,
        in_specs=[VMEM_SPEC] * (len(blocks) + 1),
        out_specs=VMEM_SPEC,
        out_shape=jax.ShapeDtypeStruct((2 * len(blocks), J, 8, SOURCES), BF16),
        compiler_params=pltpu.CompilerParams(vmem_limit_bytes=8 << 20),
        cost_estimate=cost(4 * J * 64 * SOURCES * R, 2 << 20),
        name="forward_near",
    )(*blocks, kern)


def forward_body(me, near, *refs):
    *blocks, kern, out = refs
    place = places(me[0])
    for index, rel in enumerate(NEAR):
        for half in range(2):
            out[2 * place[rel] + half] = near[2 * index + half]

    def step(j, carry):
        waves = waves_of(blocks, kern, j)
        for index, rel in enumerate(REMOTE):
            for half in range(2):
                out[2 * place[rel] + half, j] = waves[index, half]
        return carry

    lax.fori_loop(0, J, step, 0)


def forward(me, near, blocks, kern):
    return pl.pallas_call(
        forward_body,
        in_specs=[SMEM_SPEC] + [VMEM_SPEC] * (len(blocks) + 2),
        out_specs=VMEM_SPEC,
        out_shape=jax.ShapeDtypeStruct((NFREQ, J, 8, SOURCES), BF16),
        compiler_params=pltpu.CompilerParams(vmem_limit_bytes=8 << 20),
        cost_estimate=cost(4 * J * 64 * SOURCES * R, 2 << 20),
        name="forward",
    )(me, near, *blocks, kern)


def terms_of(place, field_ref, held, which, outs, j):
    field = jnp.concatenate(
        [field_ref[2 * place[rel] + half, j] for rel in which for half in range(2)], axis=0
    )
    by_real = jnp.dot(field, held[0, j], preferred_element_type=F32)
    by_imag = jnp.dot(field, held[1, j], preferred_element_type=F32)
    terms = (by_real + swapped(by_imag, -1.0)).astype(BF16)
    for index in range(len(which)):
        outs[index][j] = terms[index * 16 : index * 16 + 16]


def adjoint_remote_body(me, field_ref, kern, *refs):
    *outs, held, sems = refs
    place = places(me[0])

    def copies(j):
        return [
            pltpu.make_async_copy(kern.at[part, j], held.at[part, j], sems.at[part, j])
            for part in range(2)
        ]

    for j in range(J):
        for copy in copies(j):
            copy.start()

    def step(j, carry):
        for copy in copies(j):
            copy.wait()
        terms_of(place, field_ref, held, REMOTE, outs, j)
        return carry

    lax.fori_loop(0, J, step, 0)


def adjoint_remote(me, field, kern):
    term = jax.ShapeDtypeStruct((J, 2 * POINTS, R), BF16)
    *terms, held = pl.pallas_call(
        adjoint_remote_body,
        in_specs=[SMEM_SPEC, VMEM_SPEC, HBM_SPEC],
        out_specs=[VMEM_SPEC] * (len(REMOTE) + 1),
        out_shape=[term] * len(REMOTE) + [pltpu.VMEM(kern.shape, BF16)],
        scratch_shapes=[pltpu.SemaphoreType.DMA((2, J))],
        compiler_params=pltpu.CompilerParams(vmem_limit_bytes=8 << 20),
        cost_estimate=cost(4 * J * 64 * SOURCES * R, 14 << 20),
        name="adjoint_remote",
    )(me, field, kern)
    return terms, held


def adjoint_near_body(me, field_ref, held, *outs):
    place = places(me[0])

    def step(j, carry):
        terms_of(place, field_ref, held, NEAR, outs, j)
        return carry

    lax.fori_loop(0, J, step, 0)


def adjoint_near(me, field, held):
    return pl.pallas_call(
        adjoint_near_body,
        in_specs=[SMEM_SPEC, VMEM_SPEC, VMEM_SPEC],
        out_specs=[VMEM_SPEC] * len(NEAR),
        out_shape=[jax.ShapeDtypeStruct((J, 2 * POINTS, R), BF16)] * len(NEAR),
        compiler_params=pltpu.CompilerParams(vmem_limit_bytes=8 << 20),
        cost_estimate=cost(4 * J * 64 * SOURCES * R, 2 << 20),
        name="adjoint_near",
    )(me, field, held)


def fold_body(*refs):
    *terms, out = refs
    low = lax.broadcasted_iota(jnp.int32, (8, 128), 1) < RECV

    def step(j, carry):
        total = functools.reduce(lambda a, b: a + b, [t[j].astype(F32) for t in terms])
        for pair in range(NFREQ // 2):
            first = total[:8, pair * 128 : pair * 128 + 128]
            second = total[8:, pair * 128 : pair * 128 + 128]
            out[2 * pair, j] = jnp.where(low, first, pltpu.roll(second, RECV, 1)).astype(BF16)
            out[2 * pair + 1, j] = jnp.where(low, pltpu.roll(first, RECV, 1), second).astype(BF16)
        return carry

    lax.fori_loop(0, J, step, 0)


def fold(terms):
    return pl.pallas_call(
        fold_body,
        in_specs=[VMEM_SPEC] * len(terms),
        out_specs=VMEM_SPEC,
        out_shape=jax.ShapeDtypeStruct((NFREQ, J, 8, 128), BF16),
        compiler_params=pltpu.CompilerParams(vmem_limit_bytes=8 << 20),
        cost_estimate=cost(0, 2 << 20),
        name="fold",
    )(*terms)


def truncate_body(waves, table, onset, up, back, wide_in, wide_out):
    step = pl.program_id(0)
    last = pl.num_programs(0) - 1

    @pl.when(step == 0)
    def _():
        for half in range(SOURCES // 128):
            wide_in[half] = waves[:, half * 128 : half * 128 + 128].astype(F32)

    every = pl.ds(step, ROWS, stride=UP_POINTS)
    mine = jnp.concatenate(
        [wide_in.at[half][every, :] for half in range(SOURCES // 128)], axis=1
    ).astype(BF16)
    signal = lax.dot_general(mine, table[...], TN_DIMS, preferred_element_type=F32) * SCALE
    sample = lax.broadcasted_iota(jnp.int32, signal.shape, 1)
    kept = jnp.where(sample < onset[...], signal, 0.0).astype(BF16)
    up[...] = kept
    bins = lax.dot_general(table[...], kept, NT_DIMS, preferred_element_type=F32)
    for half in range(SOURCES // 128):
        wide_out.at[half][every, :] = bins[:, half * 128 : half * 128 + 128]

    @pl.when(step == last)
    def _():
        for half in range(SOURCES // 128):
            back[:, half * 128 : half * 128 + 128] = wide_out[half].astype(BF16)


def truncate(waves, table, onset):
    rows = waves.shape[0]
    return pl.pallas_call(
        truncate_body,
        grid=(UP_POINTS,),
        in_specs=[
            pl.BlockSpec((rows, SOURCES), lambda i: (0, 0)),
            pl.BlockSpec((ROWS, NT), lambda i: (0, 0)),
            pl.BlockSpec((SOURCES, 1), lambda i: (i, 0)),
        ],
        out_specs=[
            pl.BlockSpec((SOURCES, NT), lambda i: (i, 0)),
            pl.BlockSpec((rows, SOURCES), lambda i: (0, 0)),
        ],
        out_shape=[
            jax.ShapeDtypeStruct((UP_POINTS * SOURCES, NT), BF16),
            jax.ShapeDtypeStruct((rows, SOURCES), BF16),
        ],
        scratch_shapes=[pltpu.VMEM((SOURCES // 128, rows, 128), F32)] * 2,
        compiler_params=params(),
        cost_estimate=cost(4 * UP_POINTS * SOURCES * NT * ROWS, 8 << 20),
        name="truncate",
    )(waves, table, onset)


def update_body(bins, table, direct, onset, out, wide):
    step = pl.program_id(0)

    @pl.when(step == 0)
    def _():
        wide[...] = bins[...].astype(F32)

    mine = wide[pl.ds(step, ROWS, stride=UP_POINTS), :].astype(BF16)
    trace = lax.dot_general(mine, table[...], TN_DIMS, preferred_element_type=F32) * SCALE
    sample = lax.broadcasted_iota(jnp.int32, trace.shape, 1)
    cut = jnp.where(sample < onset[...].reshape(2 * RECV, 1), trace, 0.0)
    value = (direct[...].reshape(2 * RECV, NT).astype(F32) - cut).astype(BF16)
    out[...] = value.reshape(out.shape)


def update(bins, table, direct, onset):
    rows = bins.shape[0]
    return pl.pallas_call(
        update_body,
        grid=(UP_POINTS,),
        in_specs=[
            pl.BlockSpec((rows, 2 * RECV), lambda i: (0, 0)),
            pl.BlockSpec((ROWS, NT), lambda i: (0, 0)),
            pl.BlockSpec((2, 1, RECV, NT), lambda i: (0, i, 0, 0)),
            pl.BlockSpec((2, 1, RECV, 1), lambda i: (0, i, 0, 0)),
        ],
        out_specs=pl.BlockSpec((2, 1, RECV, NT), lambda i: (0, i, 0, 0)),
        out_shape=jax.ShapeDtypeStruct((2, UP_POINTS, RECV, NT), BF16),
        scratch_shapes=[pltpu.VMEM((rows, 2 * RECV), F32)],
        compiler_params=params(),
        cost_estimate=cost(2 * POINTS * RECV * NT * ROWS, 6 << 20),
        name="update",
    )(bins, table, direct, onset)


def shift(value, dy, dz):
    pairs = [
        (2 * y + z, 2 * ((y + dy) % NY) + (z + dz) % 2) for y in range(NY) for z in range(2)
    ]
    return lax.ppermute(value, "src", pairs)


def add(*terms):
    return functools.reduce(lambda a, b: a + b, [t.astype(F32) for t in terms]).astype(BF16)


def exchange(value):
    return lax.all_to_all(value, "freq", split_axis=0, concat_axis=0, tiled=True)


def whole(focusing, direct, kernel, onset_up, onset_back):
    me = lax.axis_index("src").reshape(1)
    up_onset = onset_up.reshape(-1, 1)
    back_onset = onset_back.reshape(2, UP_POINTS, RECV, 1)
    kernel = pltpu.with_memory_space_constraint(kernel, pltpu.HBM)

    table, bins = spectrum(
        pltpu.with_memory_space_constraint(focusing.reshape(POINTS * RECV, NT), pltpu.HBM)
    )
    bins, me, up_onset, back_onset = lax.optimization_barrier((bins, me, up_onset, back_onset))
    bins = exchange(bins.reshape(NFREQ, BLOCK, POINTS * RECV))
    own = bins.reshape(NFREQ, J, 2, 2, UP_POINTS, RECV).transpose(1, 3, 2, 4, 0, 5)
    own = own.reshape(J, 2 * POINTS, R)
    own, late_kernel = lax.optimization_barrier((own, kernel))

    across = shift(own, 0, 1)
    up = shift(own, 1, 0)
    down = shift(own, -1, 0)
    held = hold(pltpu.with_memory_space_constraint(late_kernel, pltpu.HBM))
    across_down = shift(across, -1, 0)
    across_up = shift(across, 1, 0)
    far = shift(up, 1, 0)
    across_far = shift(across_down, -1, 0)
    near = forward_near([own, up, down, across], held)
    waves = exchange(forward(me, near, [far, across_up, across_down, across_far], held))

    upgoing, back = truncate(waves.reshape(NFREQ * J * 8, SOURCES), table, up_onset)
    back = exchange(back.reshape(NFREQ, J, 8, SOURCES))

    (far, across_up, across_down, across_far), held = adjoint_remote(me, back, kernel)
    own, up, down, across = adjoint_near(me, back, held)
    r1 = shift(across_far, 1, 0)
    r5 = shift(far, -1, 0)
    r3 = shift(across_up, -1, 0)
    r2 = shift(add(across_down, r1), 1, 0)
    r6 = shift(add(up, r5), -1, 0)
    r4 = shift(add(across, r2, r3), 0, 1)
    r7 = shift(down, 1, 0)
    summed = exchange(fold([own, r6, r7, r4]))

    updated = update(
        summed.reshape(NFREQ * J * 8, 2 * RECV),
        table,
        direct.reshape(2, UP_POINTS, RECV, NT),
        back_onset,
    )
    return (
        upgoing.reshape(UP_POINTS, SOURCES, NT),
        updated.reshape(POINTS, RECV, NT),
    )


def solution(mesh):
    placed = (
        P("src", "freq", None),
        P("src", "freq", None),
        P(None, "freq", "src", None),
        P("freq", "src"),
        P("src", "freq"),
    )
    return jax.shard_map(
        whole,
        mesh=mesh,
        in_specs=placed,
        out_specs=(P("freq", "src", None), P("src", "freq", None)),
        check_vma=False,
    )
```

```python
import functools
import math

import jax
import jax.numpy as jnp
from jax import lax
from jax.experimental import pallas as pl
from jax.experimental.pallas import tpu as pltpu
from jax.sharding import PartitionSpec as P


NT = 2048
NF = 192
BIN0 = 16
NFREQ = 16
NSRC = 8
NY = 4
J = NF // NFREQ
BANDS = 2
J2 = J // BANDS
ROWS = 2 * NF // BANDS
WIDE = 4 * ROWS
PART = WIDE // NFREQ
HT = NT // 2
POINTS = 8
UP_POINTS = 4
RECV = 64
R = NFREQ * RECV
SOURCES = 256
SCALE = 2.0 / NT
F32 = jnp.float32
BF16 = jnp.bfloat16


NT_DIMS = (((1,), (1,)), ((), ()))
TN_DIMS = (((0,), (0,)), ((), ()))

OWN, UP, DOWN, FAR, ACROSS, ACROSS_UP, ACROSS_DOWN, ACROSS_FAR = range(8)
RELATIVE = ((0, 0), (3, 0), (1, 0), (2, 0), (0, 1), (3, 1), (1, 1), (2, 1))
NEAR = (OWN, UP, DOWN, ACROSS)
REMOTE = (FAR, ACROSS_UP, ACROSS_DOWN, ACROSS_FAR)


VMEM_SPEC = pl.BlockSpec(memory_space=pltpu.VMEM)
SMEM_SPEC = pl.BlockSpec(memory_space=pltpu.SMEM)
HBM_SPEC = pl.BlockSpec(memory_space=pltpu.HBM)


def params(limit=24):
    return pltpu.CompilerParams(
        dimension_semantics=("arbitrary",), vmem_limit_bytes=limit << 20
    )


def cost(flops, bytes_accessed):
    return pl.CostEstimate(flops=flops, bytes_accessed=bytes_accessed, transcendentals=0)


def turn(phase):
    quarter = (phase + NT // 8) >> 9
    rest = (phase - (quarter << 9)).astype(F32) * (2.0 * math.pi / NT)
    square = rest * rest
    sine = rest * (
        1.0 + square * (-1.0 / 6 + square * (1.0 / 120 + square * (-1.0 / 5040 + square / 362880)))
    )
    cosine = 1.0 + square * (
        -0.5 + square * (1.0 / 24 + square * (-1.0 / 720 + square * (1.0 / 40320 - square / 3628800)))
    )
    odd = (quarter & 1) == 1
    first, second = jnp.where(odd, sine, cosine), jnp.where(odd, cosine, sine)
    behind = ((quarter + 1) & 2) == 2
    below = (quarter & 2) == 2
    return jnp.where(behind, -first, first), jnp.where(below, -second, second)


def write_table(table):
    lane = lax.broadcasted_iota(jnp.int32, (ROWS, 128), 1)
    row = lax.broadcasted_iota(jnp.int32, (ROWS, 128), 0)
    quarter = row & 1
    for parity in range(BANDS):
        bin_index = BIN0 + parity + row - quarter
        fine_cos, fine_sin = turn((lane * bin_index) & (NT - 1))
        coarse_cos, coarse_sin = turn(((lane * bin_index + 4 * quarter) & 15) << 7)
        for a in range(HT // 128):
            value = coarse_cos[:, a : a + 1] * fine_cos - coarse_sin[:, a : a + 1] * fine_sin
            table[parity, :, a * 128 : (a + 1) * 128] = value.astype(BF16)


def forward_bands(table, early, late):
    for parity, mixed in enumerate((early + late, early - late)):
        yield parity, lax.dot_general(
            table[parity], mixed.astype(BF16), NT_DIMS, preferred_element_type=F32
        )


def inverse_bands(table, bands):
    even, odd = [
        lax.dot_general(bands[p], table[p], TN_DIMS, preferred_element_type=F32)
        for p in range(BANDS)
    ]
    return (even + odd) * SCALE, (even - odd) * SCALE


def spectrum_body(traces, table, out, wide):
    step = pl.program_id(0)

    @pl.when(step == 0)
    def _():
        write_table(table)

    rows = traces[...].reshape(2 * RECV, NT).astype(F32)
    for parity, bins in forward_bands(table, rows[:, :HT], rows[:, HT:]):
        wide.at[parity][pl.ds(step, ROWS, stride=UP_POINTS), :] = bins

    @pl.when(step == pl.num_programs(0) - 1)
    def _():
        for parity in range(BANDS):
            for f in range(NFREQ):
                out[f, parity] = wide[parity, f * PART : f * PART + PART].astype(BF16)


def spectrum(traces):
    return pl.pallas_call(
        spectrum_body,
        grid=(UP_POINTS,),
        in_specs=[pl.BlockSpec((2, 1, RECV, NT), lambda i: (0, i, 0, 0))],
        out_specs=[
            pl.BlockSpec((BANDS, ROWS, HT), lambda i: (0, 0, 0)),
            pl.BlockSpec((NFREQ, BANDS, PART, 128), lambda i: (0, 0, 0, 0)),
        ],
        out_shape=[
            jax.ShapeDtypeStruct((BANDS, ROWS, HT), BF16),
            jax.ShapeDtypeStruct((NFREQ, BANDS, PART, 128), BF16),
        ],
        scratch_shapes=[pltpu.VMEM((BANDS, WIDE, 128), F32)],
        compiler_params=params(),
        cost_estimate=cost(POINTS * RECV * NT * 2 * ROWS, 4 << 20),
        name="spectrum",
    )(traces)


def unfold_body(bins, out):
    low = lax.broadcasted_iota(jnp.int32, (8, 128), 1) < RECV

    def step(j, carry):
        for pair in range(NFREQ // 2):
            even = bins[2 * pair, j].astype(F32)
            odd = bins[2 * pair + 1, j].astype(F32)
            first = jnp.where(low, even, pltpu.roll(odd, RECV, 1))
            second = jnp.where(low, pltpu.roll(even, RECV, 1), odd)
            both = jnp.concatenate([first, second], axis=0).astype(BF16)
            out[j, :, pair * 128 : pair * 128 + 128] = both
        return carry

    lax.fori_loop(0, J, step, 0)


def unfold(bins):
    return pl.pallas_call(
        unfold_body,
        in_specs=[VMEM_SPEC],
        out_specs=VMEM_SPEC,
        out_shape=jax.ShapeDtypeStruct((J, 2 * POINTS, R), BF16),
        compiler_params=pltpu.CompilerParams(vmem_limit_bytes=8 << 20),
        cost_estimate=cost(0, 1 << 20),
        name="unfold",
    )(bins)


def swapped(value, sign):
    rows, lanes = value.shape
    tiles = value.reshape(rows // 8, 2, 4, lanes)
    return jnp.concatenate([-sign * tiles[:, 1:], sign * tiles[:, :1]], axis=1).reshape(rows, lanes)


def places(me):
    y, z = me // 2, me % 2
    return [2 * ((y + dy) % NY) + (z + dz) % 2 for dy, dz in RELATIVE]


def hold_body(kern, held, sems):
    copies = [
        pltpu.make_async_copy(kern.at[part], held.at[part], sems.at[part]) for part in range(2)
    ]
    for copy in copies:
        copy.start()
    for copy in copies:
        copy.wait()


def hold(kern):
    return pl.pallas_call(
        hold_body,
        in_specs=[HBM_SPEC],
        out_specs=pl.BlockSpec(memory_space=pl.ANY),
        out_shape=pltpu.VMEM(kern.shape, BF16),
        scratch_shapes=[pltpu.SemaphoreType.DMA((2,))],
        compiler_params=pltpu.CompilerParams(vmem_limit_bytes=1 << 20),
        cost_estimate=cost(0, 13 << 20),
        name="hold",
    )(kern)


def forward_body(me, *refs):
    *blocks, kern, out = refs
    place = places(me[0])

    def step(j2, carry):
        for parity in range(BANDS):
            j = parity * J2 + j2
            at = BANDS * j2 + parity
            field = jnp.concatenate([b[j] for b in blocks], axis=0)
            by_real = lax.dot_general(field, kern[0, at], NT_DIMS, preferred_element_type=F32)
            by_imag = lax.dot_general(field, kern[1, at], NT_DIMS, preferred_element_type=F32)
            waves = (by_real + swapped(by_imag, 1.0)).astype(BF16).reshape(NSRC, 2, 8, SOURCES)
            for rel in range(NSRC):
                for half in range(2):
                    out[2 * place[rel] + half, j] = waves[rel, half]
        return carry

    lax.fori_loop(0, J2, step, 0)


def forward(me, blocks, kern):
    return pl.pallas_call(
        forward_body,
        in_specs=[SMEM_SPEC] + [VMEM_SPEC] * (NSRC + 1),
        out_specs=VMEM_SPEC,
        out_shape=jax.ShapeDtypeStruct((NFREQ, J, 8, SOURCES), BF16),
        compiler_params=pltpu.CompilerParams(vmem_limit_bytes=8 << 20),
        cost_estimate=cost(8 * J * 64 * SOURCES * R, 4 << 20),
        name="forward",
    )(me, *blocks, kern)


def terms_of(place, field_ref, held, which, outs, j2, parity):
    j = parity * J2 + j2
    at = BANDS * j2 + parity
    field = jnp.concatenate(
        [field_ref[2 * place[rel] + half, j] for rel in which for half in range(2)], axis=0
    )
    by_real = jnp.dot(field, held[0, at], preferred_element_type=F32)
    by_imag = jnp.dot(field, held[1, at], preferred_element_type=F32)
    terms = (by_real + swapped(by_imag, -1.0)).astype(BF16)
    for index in range(len(which)):
        outs[index][j] = terms[index * 16 : index * 16 + 16]


def adjoint_remote_body(me, field_ref, kern, *refs):
    *outs, held, sems = refs
    place = places(me[0])

    def copies(at):
        return [
            pltpu.make_async_copy(kern.at[part, at], held.at[part, at], sems.at[part, at])
            for part in range(2)
        ]

    for at in range(J):
        for copy in copies(at):
            copy.start()

    def step(j2, carry):
        for parity in range(BANDS):
            for copy in copies(BANDS * j2 + parity):
                copy.wait()
            terms_of(place, field_ref, held, REMOTE, outs, j2, parity)
        return carry

    lax.fori_loop(0, J2, step, 0)


def adjoint_remote(me, field, kern):
    term = jax.ShapeDtypeStruct((J, 2 * POINTS, R), BF16)
    *terms, held = pl.pallas_call(
        adjoint_remote_body,
        in_specs=[SMEM_SPEC, VMEM_SPEC, HBM_SPEC],
        out_specs=[VMEM_SPEC] * (len(REMOTE) + 1),
        out_shape=[term] * len(REMOTE) + [pltpu.VMEM(kern.shape, BF16)],
        scratch_shapes=[pltpu.SemaphoreType.DMA((2, J))],
        compiler_params=pltpu.CompilerParams(vmem_limit_bytes=8 << 20),
        cost_estimate=cost(4 * J * 64 * SOURCES * R, 14 << 20),
        name="adjoint_remote",
    )(me, field, kern)
    return terms, held


def adjoint_near_body(me, field_ref, held, *outs):
    place = places(me[0])

    def step(j2, carry):
        for parity in range(BANDS):
            terms_of(place, field_ref, held, NEAR, outs, j2, parity)
        return carry

    lax.fori_loop(0, J2, step, 0)


def adjoint_near(me, field, held):
    return pl.pallas_call(
        adjoint_near_body,
        in_specs=[SMEM_SPEC, VMEM_SPEC, VMEM_SPEC],
        out_specs=[VMEM_SPEC] * len(NEAR),
        out_shape=[jax.ShapeDtypeStruct((J, 2 * POINTS, R), BF16)] * len(NEAR),
        compiler_params=pltpu.CompilerParams(vmem_limit_bytes=8 << 20),
        cost_estimate=cost(4 * J * 64 * SOURCES * R, 2 << 20),
        name="adjoint_near",
    )(me, field, held)


def fold_body(*refs):
    *terms, out = refs
    low = lax.broadcasted_iota(jnp.int32, (8, 128), 1) < RECV

    def step(j, carry):
        total = functools.reduce(lambda a, b: a + b, [t[j].astype(F32) for t in terms])
        for pair in range(NFREQ // 2):
            first = total[:8, pair * 128 : pair * 128 + 128]
            second = total[8:, pair * 128 : pair * 128 + 128]
            out[2 * pair, j] = jnp.where(low, first, pltpu.roll(second, RECV, 1)).astype(BF16)
            out[2 * pair + 1, j] = jnp.where(low, pltpu.roll(first, RECV, 1), second).astype(BF16)
        return carry

    lax.fori_loop(0, J, step, 0)


def fold(terms):
    return pl.pallas_call(
        fold_body,
        in_specs=[VMEM_SPEC] * len(terms),
        out_specs=VMEM_SPEC,
        out_shape=jax.ShapeDtypeStruct((NFREQ, J, 8, 128), BF16),
        compiler_params=pltpu.CompilerParams(vmem_limit_bytes=8 << 20),
        cost_estimate=cost(0, 2 << 20),
        name="fold",
    )(*terms)


LANES = [slice(half * 128, half * 128 + 128) for half in range(SOURCES // 128)]


def parts():
    for parity in range(BANDS):
        for f in range(NFREQ):
            start = (f * BANDS + parity) * PART
            yield parity, slice(f * PART, f * PART + PART), slice(start, start + PART)


def truncate_body(waves, table, onset, up, back, wide_in, wide_out):
    step = pl.program_id(0)

    @pl.when(step == 0)
    def _():
        for parity, inner, outer in parts():
            for half, lanes in enumerate(LANES):
                wide_in[parity, half, inner] = waves[outer, lanes].astype(F32)

    every = pl.ds(step, ROWS, stride=UP_POINTS)
    bands = [
        jnp.concatenate(
            [wide_in.at[parity, half][every, :] for half in range(len(LANES))], axis=1
        ).astype(BF16)
        for parity in range(BANDS)
    ]
    limit = onset[pl.ds(step, 1), :].astype(F32)
    limit = jnp.broadcast_to(limit, (128, SOURCES)).T[:, :1].astype(jnp.int32)
    sample = lax.broadcasted_iota(jnp.int32, (SOURCES, HT), 1)
    kept = []
    for half, signal in enumerate(inverse_bands(table, bands)):
        kept.append(jnp.where(sample < limit - half * HT, signal, 0.0).astype(BF16))
        up[:, half * HT : half * HT + HT] = kept[-1]
    for parity, bins in forward_bands(table, kept[0].astype(F32), kept[1].astype(F32)):
        for half, lanes in enumerate(LANES):
            wide_out.at[parity, half][every, :] = bins[:, lanes]

    @pl.when(step == pl.num_programs(0) - 1)
    def _():
        for parity, inner, outer in parts():
            for half, lanes in enumerate(LANES):
                back[outer, lanes] = wide_out[parity, half, inner].astype(BF16)


def truncate(waves, table, onset):
    rows = waves.shape[0]
    return pl.pallas_call(
        truncate_body,
        grid=(UP_POINTS,),
        in_specs=[
            pl.BlockSpec((rows, SOURCES), lambda i: (0, 0)),
            pl.BlockSpec((BANDS, ROWS, HT), lambda i: (0, 0, 0)),
            pl.BlockSpec((UP_POINTS, SOURCES), lambda i: (0, 0)),
        ],
        out_specs=[
            pl.BlockSpec((SOURCES, NT), lambda i: (i, 0)),
            pl.BlockSpec((rows, SOURCES), lambda i: (0, 0)),
        ],
        out_shape=[
            jax.ShapeDtypeStruct((UP_POINTS * SOURCES, NT), BF16),
            jax.ShapeDtypeStruct((rows, SOURCES), BF16),
        ],
        scratch_shapes=[pltpu.VMEM((BANDS, len(LANES), WIDE, 128), F32)] * 2,
        compiler_params=params(),
        cost_estimate=cost(2 * UP_POINTS * SOURCES * NT * 2 * ROWS, 8 << 20),
        name="truncate",
    )(waves, table, onset)


def update_body(bins, table, direct, onset, out, wide):
    step = pl.program_id(0)

    @pl.when(step == 0)
    def _():
        for parity, inner, outer in parts():
            wide[parity, inner] = bins[outer, :].astype(F32)

    every = pl.ds(step, ROWS, stride=UP_POINTS)
    bands = [wide.at[parity][every, :].astype(BF16) for parity in range(BANDS)]
    limit = onset[...].reshape(2 * RECV, 1)
    sample = lax.broadcasted_iota(jnp.int32, (2 * RECV, HT), 1)
    for half, trace in enumerate(inverse_bands(table, bands)):
        span = slice(half * HT, half * HT + HT)
        cut = jnp.where(sample < limit - half * HT, trace, 0.0)
        before = direct[:, 0, :, span].reshape(2 * RECV, HT).astype(F32)
        out[:, 0, :, span] = (before - cut).astype(BF16).reshape(2, RECV, HT)


def update(bins, table, direct, onset):
    rows = bins.shape[0]
    return pl.pallas_call(
        update_body,
        grid=(UP_POINTS,),
        in_specs=[
            pl.BlockSpec((rows, 2 * RECV), lambda i: (0, 0)),
            pl.BlockSpec((BANDS, ROWS, HT), lambda i: (0, 0, 0)),
            pl.BlockSpec((2, 1, RECV, NT), lambda i: (0, i, 0, 0)),
            pl.BlockSpec((2, 1, RECV, 1), lambda i: (0, i, 0, 0)),
        ],
        out_specs=pl.BlockSpec((2, 1, RECV, NT), lambda i: (0, i, 0, 0)),
        out_shape=jax.ShapeDtypeStruct((2, UP_POINTS, RECV, NT), BF16),
        scratch_shapes=[pltpu.VMEM((BANDS, WIDE, 2 * RECV), F32)],
        compiler_params=params(),
        cost_estimate=cost(POINTS * RECV * NT * 2 * ROWS, 5 << 20),
        name="update",
    )(bins, table, direct, onset)


def shift(value, dy, dz):
    pairs = [
        (2 * y + z, 2 * ((y + dy) % NY) + (z + dz) % 2) for y in range(NY) for z in range(2)
    ]
    return lax.ppermute(value, "src", pairs)


def add(*terms):
    return functools.reduce(lambda a, b: a + b, [t.astype(F32) for t in terms]).astype(BF16)


def exchange(value):
    return lax.all_to_all(value, "freq", split_axis=0, concat_axis=0, tiled=True)


def whole(focusing, direct, kernel, onset_up, onset_back):
    me = lax.axis_index("src").reshape(1)
    back_onset = onset_back.reshape(2, UP_POINTS, RECV, 1)
    kernel = pltpu.with_memory_space_constraint(kernel, pltpu.HBM)

    traces = focusing.reshape(2, UP_POINTS, RECV, NT)
    table, bins = spectrum(pltpu.with_memory_space_constraint(traces, pltpu.HBM))
    bins, me, back_onset = lax.optimization_barrier((bins, me, back_onset))
    own = unfold(exchange(bins).reshape(NFREQ, J, 8, 128))
    own, late_kernel = lax.optimization_barrier((own, kernel))

    across = shift(own, 0, 1)
    up = shift(own, 1, 0)
    down = shift(own, -1, 0)
    held = hold(pltpu.with_memory_space_constraint(late_kernel, pltpu.HBM))
    across_down = shift(across, -1, 0)
    across_up = shift(across, 1, 0)
    far = shift(up, 1, 0)
    across_far = shift(across_down, -1, 0)
    blocks = [own, up, down, far, across, across_up, across_down, across_far]
    waves = exchange(forward(me, blocks, held))

    upgoing, back = truncate(waves.reshape(NFREQ * J * 8, SOURCES), table, onset_up)
    back = exchange(back.reshape(NFREQ, J, 8, SOURCES))

    (far, across_up, across_down, across_far), held = adjoint_remote(me, back, kernel)
    own, up, down, across = adjoint_near(me, back, held)
    r1 = shift(across_far, 1, 0)
    r5 = shift(far, -1, 0)
    r3 = shift(across_up, -1, 0)
    r2 = shift(add(across_down, r1), 1, 0)
    r6 = shift(add(up, r5), -1, 0)
    r4 = shift(add(across, r2, r3), 0, 1)
    r7 = shift(down, 1, 0)
    summed = exchange(fold([own, r6, r7, r4]))

    updated = update(
        summed.reshape(NFREQ * J * 8, 2 * RECV),
        table,
        direct.reshape(2, UP_POINTS, RECV, NT),
        back_onset,
    )
    return (
        upgoing.reshape(UP_POINTS, SOURCES, NT),
        updated.reshape(POINTS, RECV, NT),
    )


def solution(mesh):
    placed = (
        P("src", "freq", None),
        P("src", "freq", None),
        P(None, "freq", "src", None),
        P("freq", "src"),
        P("src", "freq"),
    )
    return jax.shard_map(
        whole,
        mesh=mesh,
        in_specs=placed,
        out_specs=(P("freq", "src", None), P("src", "freq", None)),
        check_vma=False,
    )
```

```python
import functools
import math

import jax
import jax.numpy as jnp
from jax import lax
from jax.experimental import pallas as pl
from jax.experimental.pallas import tpu as pltpu
from jax.sharding import PartitionSpec as P


NT = 2048
NF = 192
BIN0 = 16
NFREQ = 16
NSRC = 8
NY = 4
J = NF // NFREQ
BANDS = 2
J2 = J // BANDS
ROWS = 2 * NF // BANDS
WIDE = 4 * ROWS
PART = WIDE // NFREQ
HT = NT // 2
POINTS = 8
UP_POINTS = 4
RECV = 64
R = NFREQ * RECV
SOURCES = 256
SCALE = 2.0 / NT
F32 = jnp.float32
BF16 = jnp.bfloat16


NT_DIMS = (((1,), (1,)), ((), ()))
TN_DIMS = (((0,), (0,)), ((), ()))

OWN, UP, DOWN, FAR, ACROSS, ACROSS_UP, ACROSS_DOWN, ACROSS_FAR = range(8)
RELATIVE = ((0, 0), (3, 0), (1, 0), (2, 0), (0, 1), (3, 1), (1, 1), (2, 1))
NEAR = (OWN, UP, DOWN, ACROSS)
REMOTE = (FAR, ACROSS_UP, ACROSS_DOWN, ACROSS_FAR)


LIMIT = 24 << 20
VMEM_SPEC = pl.BlockSpec(memory_space=pltpu.VMEM)
SMEM_SPEC = pl.BlockSpec(memory_space=pltpu.SMEM)
HBM_SPEC = pl.BlockSpec(memory_space=pltpu.HBM)


def cost(flops, bytes_accessed):
    return pl.CostEstimate(flops=flops, bytes_accessed=bytes_accessed, transcendentals=0)


def turn(phase):
    quarter = (phase + NT // 8) >> 9
    rest = (phase - (quarter << 9)).astype(F32) * (2.0 * math.pi / NT)
    square = rest * rest
    sine = rest * (
        1.0 + square * (-1.0 / 6 + square * (1.0 / 120 + square * (-1.0 / 5040 + square / 362880)))
    )
    cosine = 1.0 + square * (
        -0.5 + square * (1.0 / 24 + square * (-1.0 / 720 + square * (1.0 / 40320 - square / 3628800)))
    )
    odd = (quarter & 1) == 1
    first, second = jnp.where(odd, sine, cosine), jnp.where(odd, cosine, sine)
    behind = ((quarter + 1) & 2) == 2
    below = (quarter & 2) == 2
    return jnp.where(behind, -first, first), jnp.where(below, -second, second)


def write_table(table):
    lane = lax.broadcasted_iota(jnp.int32, (ROWS, 128), 1)
    row = lax.broadcasted_iota(jnp.int32, (ROWS, 128), 0)
    quarter = row & 1
    for parity in range(BANDS):
        bin_index = BIN0 + parity + row - quarter
        fine_cos, fine_sin = turn((lane * bin_index) & (NT - 1))
        coarse_cos, coarse_sin = turn(((lane * bin_index + 4 * quarter) & 15) << 7)
        for a in range(HT // 128):
            value = coarse_cos[:, a : a + 1] * fine_cos - coarse_sin[:, a : a + 1] * fine_sin
            table[parity, :, a * 128 : (a + 1) * 128] = value.astype(BF16)


def forward_bands(table, early, late):
    for parity, mixed in enumerate((early + late, early - late)):
        yield parity, lax.dot_general(
            table[parity], mixed.astype(BF16), NT_DIMS, preferred_element_type=F32
        )


def inverse_bands(table, bands):
    even, odd = [
        lax.dot_general(bands[p], table[p], TN_DIMS, preferred_element_type=F32)
        for p in range(BANDS)
    ]
    return (even + odd) * SCALE, (even - odd) * SCALE


def spectrum_body(traces, table, out, rows, wide, sems):
    copies = [
        pltpu.make_async_copy(traces.at[:, p], rows.at[p], sems.at[p]) for p in range(UP_POINTS)
    ]
    for copy in copies:
        copy.start()
    write_table(table)
    for p, copy in enumerate(copies):
        copy.wait()
        early = rows[p, :, :, :HT].reshape(2 * RECV, HT).astype(F32)
        late = rows[p, :, :, HT:].reshape(2 * RECV, HT).astype(F32)
        for parity, bins in forward_bands(table, early, late):
            wide.at[parity][pl.ds(p, ROWS, stride=UP_POINTS), :] = bins
    for parity in range(BANDS):
        for f in range(NFREQ):
            out[f, parity] = wide[parity, f * PART : f * PART + PART].astype(BF16)


def spectrum(traces):
    return pl.pallas_call(
        spectrum_body,
        in_specs=[HBM_SPEC],
        out_specs=[VMEM_SPEC] * 2,
        out_shape=[
            jax.ShapeDtypeStruct((BANDS, ROWS, HT), BF16),
            jax.ShapeDtypeStruct((NFREQ, BANDS, PART, 128), BF16),
        ],
        scratch_shapes=[
            pltpu.VMEM((UP_POINTS, 2, RECV, NT), BF16),
            pltpu.VMEM((BANDS, WIDE, 128), F32),
            pltpu.SemaphoreType.DMA((UP_POINTS,)),
        ],
        compiler_params=pltpu.CompilerParams(vmem_limit_bytes=LIMIT),
        cost_estimate=cost(POINTS * RECV * NT * 2 * ROWS, 4 << 20),
        name="spectrum",
    )(traces)


def unfold_body(bins, out):
    low = lax.broadcasted_iota(jnp.int32, (8, 128), 1) < RECV

    def step(j, carry):
        for pair in range(NFREQ // 2):
            even = bins[2 * pair, j].astype(F32)
            odd = bins[2 * pair + 1, j].astype(F32)
            first = jnp.where(low, even, pltpu.roll(odd, RECV, 1))
            second = jnp.where(low, pltpu.roll(even, RECV, 1), odd)
            both = jnp.concatenate([first, second], axis=0).astype(BF16)
            out[j, :, pair * 128 : pair * 128 + 128] = both
        return carry

    lax.fori_loop(0, J, step, 0)


def unfold(bins):
    return pl.pallas_call(
        unfold_body,
        in_specs=[VMEM_SPEC],
        out_specs=VMEM_SPEC,
        out_shape=jax.ShapeDtypeStruct((J, 2 * POINTS, R), BF16),
        compiler_params=pltpu.CompilerParams(vmem_limit_bytes=8 << 20),
        cost_estimate=cost(0, 1 << 20),
        name="unfold",
    )(bins)


def swapped(value, sign):
    rows, lanes = value.shape
    tiles = value.reshape(rows // 8, 2, 4, lanes)
    return jnp.concatenate([-sign * tiles[:, 1:], sign * tiles[:, :1]], axis=1).reshape(rows, lanes)


def places(me):
    y, z = me // 2, me % 2
    return [2 * ((y + dy) % NY) + (z + dz) % 2 for dy, dz in RELATIVE]


def hold_body(kern, held, sems):
    copies = [
        pltpu.make_async_copy(kern.at[part], held.at[part], sems.at[part]) for part in range(2)
    ]
    for copy in copies:
        copy.start()
    for copy in copies:
        copy.wait()


def hold(kern):
    return pl.pallas_call(
        hold_body,
        in_specs=[HBM_SPEC],
        out_specs=pl.BlockSpec(memory_space=pl.ANY),
        out_shape=pltpu.VMEM(kern.shape, BF16),
        scratch_shapes=[pltpu.SemaphoreType.DMA((2,))],
        compiler_params=pltpu.CompilerParams(vmem_limit_bytes=1 << 20),
        cost_estimate=cost(0, 13 << 20),
        name="hold",
    )(kern)


def forward_body(me, *refs):
    *blocks, kern, out = refs
    place = places(me[0])

    def step(j2, carry):
        for parity in range(BANDS):
            j = parity * J2 + j2
            at = BANDS * j2 + parity
            field = jnp.concatenate([b[j] for b in blocks], axis=0).T
            by_real = jnp.dot(kern[0, at], field, preferred_element_type=F32).T
            by_imag = jnp.dot(kern[1, at], field, preferred_element_type=F32).T
            waves = (by_real + swapped(by_imag, 1.0)).astype(BF16).reshape(NSRC, 2, 8, SOURCES)
            for rel in range(NSRC):
                for half in range(2):
                    out[2 * place[rel] + half, j] = waves[rel, half]
        return carry

    lax.fori_loop(0, J2, step, 0)


def forward(me, blocks, kern):
    return pl.pallas_call(
        forward_body,
        in_specs=[SMEM_SPEC] + [VMEM_SPEC] * (NSRC + 1),
        out_specs=VMEM_SPEC,
        out_shape=jax.ShapeDtypeStruct((NFREQ, J, 8, SOURCES), BF16),
        compiler_params=pltpu.CompilerParams(vmem_limit_bytes=8 << 20),
        cost_estimate=cost(8 * J * 64 * SOURCES * R, 4 << 20),
        name="forward",
    )(me, *blocks, kern)


def terms_of(place, field_ref, held, which, outs, j2, parity):
    j = parity * J2 + j2
    at = BANDS * j2 + parity
    field = jnp.concatenate(
        [field_ref[2 * place[rel] + half, j] for rel in which for half in range(2)], axis=0
    )
    by_real = jnp.dot(field, held[0, at], preferred_element_type=F32)
    by_imag = jnp.dot(field, held[1, at], preferred_element_type=F32)
    terms = (by_real + swapped(by_imag, -1.0)).astype(BF16)
    for index in range(len(which)):
        outs[index][j] = terms[index * 16 : index * 16 + 16]


def adjoint_remote_body(me, field_ref, kern, *refs):
    *outs, held, sems = refs
    place = places(me[0])

    def copies(at):
        return [
            pltpu.make_async_copy(kern.at[part, at], held.at[part, at], sems.at[part, at])
            for part in range(2)
        ]

    for at in range(J):
        for copy in copies(at):
            copy.start()

    def step(j2, carry):
        for parity in range(BANDS):
            for copy in copies(BANDS * j2 + parity):
                copy.wait()
            terms_of(place, field_ref, held, REMOTE, outs, j2, parity)
        return carry

    lax.fori_loop(0, J2, step, 0)


def adjoint_remote(me, field, kern):
    term = jax.ShapeDtypeStruct((J, 2 * POINTS, R), BF16)
    *terms, held = pl.pallas_call(
        adjoint_remote_body,
        in_specs=[SMEM_SPEC, VMEM_SPEC, HBM_SPEC],
        out_specs=[VMEM_SPEC] * (len(REMOTE) + 1),
        out_shape=[term] * len(REMOTE) + [pltpu.VMEM(kern.shape, BF16)],
        scratch_shapes=[pltpu.SemaphoreType.DMA((2, J))],
        compiler_params=pltpu.CompilerParams(vmem_limit_bytes=8 << 20),
        cost_estimate=cost(4 * J * 64 * SOURCES * R, 14 << 20),
        name="adjoint_remote",
    )(me, field, kern)
    return terms, held


def adjoint_near_body(me, field_ref, held, *outs):
    place = places(me[0])

    def step(j2, carry):
        for parity in range(BANDS):
            terms_of(place, field_ref, held, NEAR, outs, j2, parity)
        return carry

    lax.fori_loop(0, J2, step, 0)


def adjoint_near(me, field, held):
    return pl.pallas_call(
        adjoint_near_body,
        in_specs=[SMEM_SPEC, VMEM_SPEC, VMEM_SPEC],
        out_specs=[VMEM_SPEC] * len(NEAR),
        out_shape=[jax.ShapeDtypeStruct((J, 2 * POINTS, R), BF16)] * len(NEAR),
        compiler_params=pltpu.CompilerParams(vmem_limit_bytes=8 << 20),
        cost_estimate=cost(4 * J * 64 * SOURCES * R, 2 << 20),
        name="adjoint_near",
    )(me, field, held)


def fold_body(*refs):
    *terms, out = refs
    low = lax.broadcasted_iota(jnp.int32, (8, 128), 1) < RECV

    def step(j, carry):
        total = functools.reduce(lambda a, b: a + b, [t[j].astype(F32) for t in terms])
        for pair in range(NFREQ // 2):
            first = total[:8, pair * 128 : pair * 128 + 128]
            second = total[8:, pair * 128 : pair * 128 + 128]
            out[2 * pair, j] = jnp.where(low, first, pltpu.roll(second, RECV, 1)).astype(BF16)
            out[2 * pair + 1, j] = jnp.where(low, pltpu.roll(first, RECV, 1), second).astype(BF16)
        return carry

    lax.fori_loop(0, J, step, 0)


def fold(terms):
    return pl.pallas_call(
        fold_body,
        in_specs=[VMEM_SPEC] * len(terms),
        out_specs=VMEM_SPEC,
        out_shape=jax.ShapeDtypeStruct((NFREQ, J, 8, 128), BF16),
        compiler_params=pltpu.CompilerParams(vmem_limit_bytes=8 << 20),
        cost_estimate=cost(0, 2 << 20),
        name="fold",
    )(*terms)


PER = 2
LANES = [slice(half * 128, half * 128 + 128) for half in range(SOURCES // 128)]


def parts():
    for parity in range(BANDS):
        for f in range(NFREQ):
            start = (f * BANDS + parity) * PART
            yield parity, slice(f * PART, f * PART + PART), slice(start, start + PART)


def truncate_body(waves, table, onset, up, back, wide_in, wide_out, rows, sems):
    for parity, inner, outer in parts():
        for half, lanes in enumerate(LANES):
            wide_in[parity, half, inner] = waves[outer, lanes].astype(F32)
    sample = lax.broadcasted_iota(jnp.int32, (PER * SOURCES, HT), 1)
    copies = []
    for group in range(UP_POINTS // PER):
        points = [PER * group + index for index in range(PER)]
        every = [pl.ds(point, ROWS, stride=UP_POINTS) for point in points]
        bands = [
            jnp.concatenate(
                [wide_in.at[parity, half][e, :] for e in every for half in range(len(LANES))], axis=1
            ).astype(BF16)
            for parity in range(BANDS)
        ]
        limit = [
            jnp.broadcast_to(onset[p : p + 1, :].astype(F32), (128, SOURCES)).T[:, :1] for p in points
        ]
        limit = jnp.concatenate(limit, axis=0).astype(jnp.int32)
        kept = []
        for half, signal in enumerate(inverse_bands(table, bands)):
            kept.append(jnp.where(sample < limit - half * HT, signal, 0.0).astype(BF16))
            rows[group, :, half * HT : half * HT + HT] = kept[-1]
        span = pl.ds(group * PER * SOURCES, PER * SOURCES)
        copies.append(pltpu.make_async_copy(rows.at[group], up.at[span], sems.at[group]))
        copies[-1].start()
        for parity, bins in forward_bands(table, kept[0].astype(F32), kept[1].astype(F32)):
            for index, e in enumerate(every):
                for half in range(len(LANES)):
                    start = index * SOURCES + half * 128
                    wide_out.at[parity, half][e, :] = bins[:, start : start + 128]
    for parity, inner, outer in parts():
        for half, lanes in enumerate(LANES):
            back[outer, lanes] = wide_out[parity, half, inner].astype(BF16)
    for copy in copies:
        copy.wait()


def truncate(waves, table, onset):
    groups = UP_POINTS // PER
    return pl.pallas_call(
        truncate_body,
        in_specs=[VMEM_SPEC] * 3,
        out_specs=[pl.BlockSpec(memory_space=pl.ANY), VMEM_SPEC],
        out_shape=[
            pltpu.HBM((UP_POINTS * SOURCES, NT), BF16),
            jax.ShapeDtypeStruct(waves.shape, BF16),
        ],
        scratch_shapes=[pltpu.VMEM((BANDS, len(LANES), WIDE, 128), F32)] * 2
        + [
            pltpu.VMEM((groups, PER * SOURCES, NT), BF16),
            pltpu.SemaphoreType.DMA((groups,)),
        ],
        compiler_params=pltpu.CompilerParams(vmem_limit_bytes=40 << 20),
        cost_estimate=cost(2 * UP_POINTS * SOURCES * NT * 2 * ROWS, 8 << 20),
        name="truncate",
    )(waves, table, onset)


def update_body(bins, table, direct, onset, out, wide, rows, sems):
    for parity, inner, outer in parts():
        wide[parity, inner] = bins[outer, :].astype(F32)
    sample = lax.broadcasted_iota(jnp.int32, (2 * RECV, HT), 1)
    copies = []
    for p in range(UP_POINTS):
        every = pl.ds(p, ROWS, stride=UP_POINTS)
        bands = [wide.at[parity][every, :].astype(BF16) for parity in range(BANDS)]
        limit = onset[:, p].reshape(2 * RECV, 1)
        for half, trace in enumerate(inverse_bands(table, bands)):
            span = slice(half * HT, half * HT + HT)
            cut = jnp.where(sample < limit - half * HT, trace, 0.0)
            before = direct[:, p, :, span].reshape(2 * RECV, HT).astype(F32)
            rows[p, :, :, span] = (before - cut).astype(BF16).reshape(2, RECV, HT)
        copies.append(pltpu.make_async_copy(rows.at[p], out.at[:, p], sems.at[p]))
        copies[-1].start()
    for copy in copies:
        copy.wait()


def update(bins, table, direct, onset):
    return pl.pallas_call(
        update_body,
        in_specs=[VMEM_SPEC] * 4,
        out_specs=pl.BlockSpec(memory_space=pl.ANY),
        out_shape=pltpu.HBM((2, UP_POINTS, RECV, NT), BF16),
        scratch_shapes=[
            pltpu.VMEM((BANDS, WIDE, 2 * RECV), F32),
            pltpu.VMEM((UP_POINTS, 2, RECV, NT), BF16),
            pltpu.SemaphoreType.DMA((UP_POINTS,)),
        ],
        compiler_params=pltpu.CompilerParams(vmem_limit_bytes=LIMIT),
        cost_estimate=cost(POINTS * RECV * NT * 2 * ROWS, 5 << 20),
        name="update",
    )(bins, table, direct, onset)


def shift(value, dy, dz):
    pairs = [
        (2 * y + z, 2 * ((y + dy) % NY) + (z + dz) % 2) for y in range(NY) for z in range(2)
    ]
    return lax.ppermute(value, "src", pairs)


def add(*terms):
    return functools.reduce(lambda a, b: a + b, [t.astype(F32) for t in terms]).astype(BF16)


def exchange(value):
    return lax.all_to_all(value, "freq", split_axis=0, concat_axis=0, tiled=True)


def whole(focusing, direct, kernel, onset_up, onset_back):
    me = lax.axis_index("src").reshape(1)
    back_onset = onset_back.reshape(2, UP_POINTS, RECV, 1)
    kernel = pltpu.with_memory_space_constraint(kernel, pltpu.HBM)

    traces = focusing.reshape(2, UP_POINTS, RECV, NT)
    table, bins = spectrum(pltpu.with_memory_space_constraint(traces, pltpu.HBM))
    bins, me, back_onset = lax.optimization_barrier((bins, me, back_onset))
    own = unfold(exchange(bins).reshape(NFREQ, J, 8, 128))
    own, late_kernel = lax.optimization_barrier((own, kernel))

    across = shift(own, 0, 1)
    up = shift(own, 1, 0)
    down = shift(own, -1, 0)
    held = hold(pltpu.with_memory_space_constraint(late_kernel, pltpu.HBM))
    across_down = shift(across, -1, 0)
    across_up = shift(across, 1, 0)
    far = shift(up, 1, 0)
    across_far = shift(across_down, -1, 0)
    blocks = [own, up, down, far, across, across_up, across_down, across_far]
    waves = exchange(forward(me, blocks, held))

    upgoing, back = truncate(waves.reshape(NFREQ * J * 8, SOURCES), table, onset_up)
    back = exchange(back.reshape(NFREQ, J, 8, SOURCES))

    (far, across_up, across_down, across_far), held = adjoint_remote(me, back, kernel)
    own, up, down, across = adjoint_near(me, back, held)
    r1 = shift(across_far, 1, 0)
    r5 = shift(far, -1, 0)
    r3 = shift(across_up, -1, 0)
    r2 = shift(add(across_down, r1), 1, 0)
    r6 = shift(add(up, r5), -1, 0)
    r4 = shift(add(across, r2, r3), 0, 1)
    r7 = shift(down, 1, 0)
    summed = exchange(fold([own, r6, r7, r4]))

    updated = update(
        summed.reshape(NFREQ * J * 8, 2 * RECV),
        table,
        direct.reshape(2, UP_POINTS, RECV, NT),
        back_onset,
    )
    return (
        upgoing.reshape(UP_POINTS, SOURCES, NT),
        updated.reshape(POINTS, RECV, NT),
    )


def solution(mesh):
    placed = (
        P("src", "freq", None),
        P("src", "freq", None),
        P(None, "freq", "src", None),
        P("freq", "src"),
        P("src", "freq"),
    )
    return jax.shard_map(
        whole,
        mesh=mesh,
        in_specs=placed,
        out_specs=(P("freq", "src", None), P("src", "freq", None)),
        check_vma=False,
    )
```

```python
import functools
import math

import jax
import jax.numpy as jnp
from jax import lax
from jax.experimental import pallas as pl
from jax.experimental.pallas import tpu as pltpu
from jax.sharding import PartitionSpec as P


NT = 2048
NF = 192
BIN0 = 16
NFREQ = 16
NSRC = 8
NY = 4
J = NF // NFREQ
BANDS = 2
J2 = J // BANDS
ROWS = 2 * NF // BANDS
WIDE = 4 * ROWS
PART = WIDE // NFREQ
HT = NT // 2
POINTS = 8
UP_POINTS = 4
RECV = 64
R = NFREQ * RECV
SOURCES = 256
SCALE = 2.0 / NT
F32 = jnp.float32
BF16 = jnp.bfloat16


NT_DIMS = (((1,), (1,)), ((), ()))
TN_DIMS = (((0,), (0,)), ((), ()))

OWN, UP, DOWN, FAR, ACROSS, ACROSS_UP, ACROSS_DOWN, ACROSS_FAR = range(8)
RELATIVE = ((0, 0), (3, 0), (1, 0), (2, 0), (0, 1), (3, 1), (1, 1), (2, 1))
NEAR = (OWN, UP, DOWN, ACROSS)
REMOTE = (FAR, ACROSS_UP, ACROSS_DOWN, ACROSS_FAR)


LIMIT = 24 << 20
VMEM_SPEC = pl.BlockSpec(memory_space=pltpu.VMEM)
SMEM_SPEC = pl.BlockSpec(memory_space=pltpu.SMEM)
HBM_SPEC = pl.BlockSpec(memory_space=pltpu.HBM)


def cost(flops, bytes_accessed):
    return pl.CostEstimate(flops=flops, bytes_accessed=bytes_accessed, transcendentals=0)


def turn(phase):
    quarter = (phase + NT // 8) >> 9
    rest = (phase - (quarter << 9)).astype(F32) * (2.0 * math.pi / NT)
    square = rest * rest
    sine = rest * (
        1.0 + square * (-1.0 / 6 + square * (1.0 / 120 + square * (-1.0 / 5040 + square / 362880)))
    )
    cosine = 1.0 + square * (
        -0.5 + square * (1.0 / 24 + square * (-1.0 / 720 + square * (1.0 / 40320 - square / 3628800)))
    )
    odd = (quarter & 1) == 1
    first, second = jnp.where(odd, sine, cosine), jnp.where(odd, cosine, sine)
    behind = ((quarter + 1) & 2) == 2
    below = (quarter & 2) == 2
    return jnp.where(behind, -first, first), jnp.where(below, -second, second)


def write_table(table):
    lane = lax.broadcasted_iota(jnp.int32, (ROWS, 128), 1)
    row = lax.broadcasted_iota(jnp.int32, (ROWS, 128), 0)
    quarter = row & 1
    for parity in range(BANDS):
        bin_index = BIN0 + parity + row - quarter
        fine_cos, fine_sin = turn((lane * bin_index) & (NT - 1))
        coarse_cos, coarse_sin = turn(((lane * bin_index + 4 * quarter) & 15) << 7)
        for a in range(HT // 128):
            value = coarse_cos[:, a : a + 1] * fine_cos - coarse_sin[:, a : a + 1] * fine_sin
            table[parity, :, a * 128 : (a + 1) * 128] = value.astype(BF16)


def forward_bands(table, early, late):
    for parity, mixed in enumerate((early + late, early - late)):
        yield parity, lax.dot_general(
            table[parity], mixed.astype(BF16), NT_DIMS, preferred_element_type=F32
        )


def inverse_bands(table, bands):
    even, odd = [
        lax.dot_general(bands[p], table[p], TN_DIMS, preferred_element_type=F32)
        for p in range(BANDS)
    ]
    return (even + odd) * SCALE, (even - odd) * SCALE


def spectrum_body(traces, table, out, rows, wide, sems):
    copies = [
        pltpu.make_async_copy(traces.at[:, p], rows.at[p], sems.at[p]) for p in range(UP_POINTS)
    ]
    for copy in copies:
        copy.start()
    write_table(table)
    for p, copy in enumerate(copies):
        copy.wait()
        early = rows[p, :, :, :HT].reshape(2 * RECV, HT).astype(F32)
        late = rows[p, :, :, HT:].reshape(2 * RECV, HT).astype(F32)
        for parity, bins in forward_bands(table, early, late):
            wide.at[parity][pl.ds(p, ROWS, stride=UP_POINTS), :] = bins
    for parity in range(BANDS):
        for f in range(NFREQ):
            out[f, parity] = wide[parity, f * PART : f * PART + PART].astype(BF16)


def spectrum(traces):
    return pl.pallas_call(
        spectrum_body,
        in_specs=[HBM_SPEC],
        out_specs=[VMEM_SPEC] * 2,
        out_shape=[
            jax.ShapeDtypeStruct((BANDS, ROWS, HT), BF16),
            jax.ShapeDtypeStruct((NFREQ, BANDS, PART, 128), BF16),
        ],
        scratch_shapes=[
            pltpu.VMEM((UP_POINTS, 2, RECV, NT), BF16),
            pltpu.VMEM((BANDS, WIDE, 128), F32),
            pltpu.SemaphoreType.DMA((UP_POINTS,)),
        ],
        compiler_params=pltpu.CompilerParams(vmem_limit_bytes=LIMIT),
        cost_estimate=cost(POINTS * RECV * NT * 2 * ROWS, 4 << 20),
        name="spectrum",
    )(traces)


def unfold_body(bins, out):
    low = lax.broadcasted_iota(jnp.int32, (8, 128), 1) < RECV

    def step(j, carry):
        for pair in range(NFREQ // 2):
            even = bins[2 * pair, j].astype(F32)
            odd = bins[2 * pair + 1, j].astype(F32)
            first = jnp.where(low, even, pltpu.roll(odd, RECV, 1))
            second = jnp.where(low, pltpu.roll(even, RECV, 1), odd)
            both = jnp.concatenate([first, second], axis=0).astype(BF16)
            out[j, :, pair * 128 : pair * 128 + 128] = both
        return carry

    lax.fori_loop(0, J, step, 0)


def unfold(bins):
    return pl.pallas_call(
        unfold_body,
        in_specs=[VMEM_SPEC],
        out_specs=VMEM_SPEC,
        out_shape=jax.ShapeDtypeStruct((J, 2 * POINTS, R), BF16),
        compiler_params=pltpu.CompilerParams(vmem_limit_bytes=8 << 20),
        cost_estimate=cost(0, 1 << 20),
        name="unfold",
    )(bins)


def swapped(value, sign):
    rows, lanes = value.shape
    tiles = value.reshape(rows // 8, 2, 4, lanes)
    return jnp.concatenate([-sign * tiles[:, 1:], sign * tiles[:, :1]], axis=1).reshape(rows, lanes)


def places(me):
    y, z = me // 2, me % 2
    return [2 * ((y + dy) % NY) + (z + dz) % 2 for dy, dz in RELATIVE]


KEPT = 2


def hold_body(kern, held, kept, sems):
    copies = [
        pltpu.make_async_copy(kern.at[part], held.at[part], sems.at[part]) for part in range(2)
    ] + [
        pltpu.make_async_copy(kern.at[part, :KEPT], kept.at[part], sems.at[2 + part])
        for part in range(2)
    ]
    for copy in copies:
        copy.start()
    for copy in copies:
        copy.wait()


def hold(kern):
    return pl.pallas_call(
        hold_body,
        in_specs=[HBM_SPEC],
        out_specs=[pl.BlockSpec(memory_space=pl.ANY)] * 2,
        out_shape=[
            pltpu.VMEM(kern.shape, BF16),
            pltpu.VMEM((2, KEPT) + kern.shape[2:], BF16),
        ],
        scratch_shapes=[pltpu.SemaphoreType.DMA((4,))],
        compiler_params=pltpu.CompilerParams(vmem_limit_bytes=1 << 20),
        cost_estimate=cost(0, 13 << 20),
        name="hold",
    )(kern)


def forward_body(me, *refs):
    *blocks, kern, out = refs
    place = places(me[0])

    def step(j2, carry):
        for parity in range(BANDS):
            j = parity * J2 + j2
            at = BANDS * j2 + parity
            field = jnp.concatenate([b[j] for b in blocks], axis=0).T
            by_real = jnp.dot(kern[0, at], field, preferred_element_type=F32).T
            by_imag = jnp.dot(kern[1, at], field, preferred_element_type=F32).T
            waves = (by_real + swapped(by_imag, 1.0)).astype(BF16).reshape(NSRC, 2, 8, SOURCES)
            for rel in range(NSRC):
                for half in range(2):
                    out[2 * place[rel] + half, j] = waves[rel, half]
        return carry

    lax.fori_loop(0, J2, step, 0)


def forward(me, blocks, kern):
    return pl.pallas_call(
        forward_body,
        in_specs=[SMEM_SPEC] + [VMEM_SPEC] * (NSRC + 1),
        out_specs=VMEM_SPEC,
        out_shape=jax.ShapeDtypeStruct((NFREQ, J, 8, SOURCES), BF16),
        compiler_params=pltpu.CompilerParams(vmem_limit_bytes=8 << 20),
        cost_estimate=cost(8 * J * 64 * SOURCES * R, 4 << 20),
        name="forward",
    )(me, *blocks, kern)


def terms_of(place, field_ref, held, which, outs, j2, parity):
    j = parity * J2 + j2
    at = BANDS * j2 + parity
    field = jnp.concatenate(
        [field_ref[2 * place[rel] + half, j] for rel in which for half in range(2)], axis=0
    )
    by_real = jnp.dot(field, held[0, at], preferred_element_type=F32)
    by_imag = jnp.dot(field, held[1, at], preferred_element_type=F32)
    terms = (by_real + swapped(by_imag, -1.0)).astype(BF16)
    for index in range(len(which)):
        outs[index][j] = terms[index * 16 : index * 16 + 16]


def adjoint_remote_body(me, field_ref, kern, kept, *refs):
    *outs, held, sems = refs
    place = places(me[0])

    def copies(at):
        return [
            pltpu.make_async_copy(kern.at[part, at], held.at[part, at], sems.at[part, at])
            for part in range(2)
        ]

    for at in range(J):
        for part in range(2):
            source = kept if at < KEPT else kern
            pltpu.make_async_copy(
                source.at[part, at], held.at[part, at], sems.at[part, at]
            ).start()

    def step(j2, carry):
        for parity in range(BANDS):
            for copy in copies(BANDS * j2 + parity):
                copy.wait()
            terms_of(place, field_ref, held, REMOTE, outs, j2, parity)
        return carry

    lax.fori_loop(0, J2, step, 0)


def adjoint_remote(me, field, kern, kept):
    term = jax.ShapeDtypeStruct((J, 2 * POINTS, R), BF16)
    *terms, held = pl.pallas_call(
        adjoint_remote_body,
        in_specs=[SMEM_SPEC, VMEM_SPEC, HBM_SPEC, VMEM_SPEC],
        out_specs=[VMEM_SPEC] * (len(REMOTE) + 1),
        out_shape=[term] * len(REMOTE) + [pltpu.VMEM(kern.shape, BF16)],
        scratch_shapes=[pltpu.SemaphoreType.DMA((2, J))],
        compiler_params=pltpu.CompilerParams(vmem_limit_bytes=8 << 20),
        cost_estimate=cost(4 * J * 64 * SOURCES * R, 14 << 20),
        name="adjoint_remote",
    )(me, field, kern, kept)
    return terms, held


def adjoint_near_body(me, field_ref, held, *outs):
    place = places(me[0])

    def step(j2, carry):
        for parity in range(BANDS):
            terms_of(place, field_ref, held, NEAR, outs, j2, parity)
        return carry

    lax.fori_loop(0, J2, step, 0)


def adjoint_near(me, field, held):
    return pl.pallas_call(
        adjoint_near_body,
        in_specs=[SMEM_SPEC, VMEM_SPEC, VMEM_SPEC],
        out_specs=[VMEM_SPEC] * len(NEAR),
        out_shape=[jax.ShapeDtypeStruct((J, 2 * POINTS, R), BF16)] * len(NEAR),
        compiler_params=pltpu.CompilerParams(vmem_limit_bytes=8 << 20),
        cost_estimate=cost(4 * J * 64 * SOURCES * R, 2 << 20),
        name="adjoint_near",
    )(me, field, held)


def fold_body(*refs):
    *terms, out = refs
    low = lax.broadcasted_iota(jnp.int32, (8, 128), 1) < RECV

    def step(j, carry):
        total = functools.reduce(lambda a, b: a + b, [t[j].astype(F32) for t in terms])
        for pair in range(NFREQ // 2):
            first = total[:8, pair * 128 : pair * 128 + 128]
            second = total[8:, pair * 128 : pair * 128 + 128]
            out[2 * pair, j] = jnp.where(low, first, pltpu.roll(second, RECV, 1)).astype(BF16)
            out[2 * pair + 1, j] = jnp.where(low, pltpu.roll(first, RECV, 1), second).astype(BF16)
        return carry

    lax.fori_loop(0, J, step, 0)


def fold(terms):
    return pl.pallas_call(
        fold_body,
        in_specs=[VMEM_SPEC] * len(terms),
        out_specs=VMEM_SPEC,
        out_shape=jax.ShapeDtypeStruct((NFREQ, J, 8, 128), BF16),
        compiler_params=pltpu.CompilerParams(vmem_limit_bytes=8 << 20),
        cost_estimate=cost(0, 2 << 20),
        name="fold",
    )(*terms)


PER = 2
LANES = [slice(half * 128, half * 128 + 128) for half in range(SOURCES // 128)]


def parts():
    for parity in range(BANDS):
        for f in range(NFREQ):
            start = (f * BANDS + parity) * PART
            yield parity, slice(f * PART, f * PART + PART), slice(start, start + PART)


def truncate_body(waves, table, onset, up, back, wide_in, wide_out, rows, sems):
    for parity, inner, outer in parts():
        for half, lanes in enumerate(LANES):
            wide_in[parity, half, inner] = waves[outer, lanes].astype(F32)
    sample = lax.broadcasted_iota(jnp.int32, (PER * SOURCES, HT), 1)
    copies = []
    for group in range(UP_POINTS // PER):
        points = [PER * group + index for index in range(PER)]
        every = [pl.ds(point, ROWS, stride=UP_POINTS) for point in points]
        bands = [
            jnp.concatenate(
                [wide_in.at[parity, half][e, :] for e in every for half in range(len(LANES))], axis=1
            ).astype(BF16)
            for parity in range(BANDS)
        ]
        limit = [
            jnp.broadcast_to(onset[p : p + 1, :].astype(F32), (128, SOURCES)).T[:, :1] for p in points
        ]
        limit = jnp.concatenate(limit, axis=0).astype(jnp.int32)
        kept = []
        for half, signal in enumerate(inverse_bands(table, bands)):
            kept.append(jnp.where(sample < limit - half * HT, signal, 0.0).astype(BF16))
            rows[group, :, half * HT : half * HT + HT] = kept[-1]
        span = pl.ds(group * PER * SOURCES, PER * SOURCES)
        copies.append(pltpu.make_async_copy(rows.at[group], up.at[span], sems.at[group]))
        copies[-1].start()
        for parity, bins in forward_bands(table, kept[0].astype(F32), kept[1].astype(F32)):
            for index, e in enumerate(every):
                for half in range(len(LANES)):
                    start = index * SOURCES + half * 128
                    wide_out.at[parity, half][e, :] = bins[:, start : start + 128]
    for parity, inner, outer in parts():
        for half, lanes in enumerate(LANES):
            back[outer, lanes] = wide_out[parity, half, inner].astype(BF16)
    for copy in copies:
        copy.wait()


def truncate(waves, table, onset):
    groups = UP_POINTS // PER
    return pl.pallas_call(
        truncate_body,
        in_specs=[VMEM_SPEC] * 3,
        out_specs=[pl.BlockSpec(memory_space=pl.ANY), VMEM_SPEC],
        out_shape=[
            pltpu.HBM((UP_POINTS * SOURCES, NT), BF16),
            jax.ShapeDtypeStruct(waves.shape, BF16),
        ],
        scratch_shapes=[pltpu.VMEM((BANDS, len(LANES), WIDE, 128), F32)] * 2
        + [
            pltpu.VMEM((groups, PER * SOURCES, NT), BF16),
            pltpu.SemaphoreType.DMA((groups,)),
        ],
        compiler_params=pltpu.CompilerParams(vmem_limit_bytes=40 << 20),
        cost_estimate=cost(2 * UP_POINTS * SOURCES * NT * 2 * ROWS, 8 << 20),
        name="truncate",
    )(waves, table, onset)


def update_body(bins, table, direct, onset, out, wide, rows, sems):
    for parity, inner, outer in parts():
        wide[parity, inner] = bins[outer, :].astype(F32)
    sample = lax.broadcasted_iota(jnp.int32, (2 * RECV, HT), 1)
    copies = []
    for p in range(UP_POINTS):
        every = pl.ds(p, ROWS, stride=UP_POINTS)
        bands = [wide.at[parity][every, :].astype(BF16) for parity in range(BANDS)]
        row = jnp.concatenate([onset[p : p + 1, :], onset[p + 4 : p + 5, :]], axis=1).astype(F32)
        limit = jnp.broadcast_to(row, (128, 2 * RECV)).T[:, :1].astype(jnp.int32)
        for half, trace in enumerate(inverse_bands(table, bands)):
            span = slice(half * HT, half * HT + HT)
            cut = jnp.where(sample < limit - half * HT, trace, 0.0)
            before = direct[:, p, :, span].reshape(2 * RECV, HT).astype(F32)
            rows[p, :, :, span] = (before - cut).astype(BF16).reshape(2, RECV, HT)
        copies.append(pltpu.make_async_copy(rows.at[p], out.at[:, p], sems.at[p]))
        copies[-1].start()
    for copy in copies:
        copy.wait()


def update(bins, table, direct, onset):
    return pl.pallas_call(
        update_body,
        in_specs=[VMEM_SPEC] * 4,
        out_specs=pl.BlockSpec(memory_space=pl.ANY),
        out_shape=pltpu.HBM((2, UP_POINTS, RECV, NT), BF16),
        scratch_shapes=[
            pltpu.VMEM((BANDS, WIDE, 2 * RECV), F32),
            pltpu.VMEM((UP_POINTS, 2, RECV, NT), BF16),
            pltpu.SemaphoreType.DMA((UP_POINTS,)),
        ],
        compiler_params=pltpu.CompilerParams(vmem_limit_bytes=LIMIT),
        cost_estimate=cost(POINTS * RECV * NT * 2 * ROWS, 5 << 20),
        name="update",
    )(bins, table, direct, onset)


def shift(value, dy, dz):
    pairs = [
        (2 * y + z, 2 * ((y + dy) % NY) + (z + dz) % 2) for y in range(NY) for z in range(2)
    ]
    return lax.ppermute(value, "src", pairs)


def add(*terms):
    return functools.reduce(lambda a, b: a + b, [t.astype(F32) for t in terms]).astype(BF16)


def exchange(value):
    return lax.all_to_all(value, "freq", split_axis=0, concat_axis=0, tiled=True)


def whole(focusing, direct, kernel, onset_up, onset_back):
    me = lax.axis_index("src").reshape(1)
    kernel = pltpu.with_memory_space_constraint(kernel, pltpu.HBM)

    traces = focusing.reshape(2, UP_POINTS, RECV, NT)
    table, bins = spectrum(pltpu.with_memory_space_constraint(traces, pltpu.HBM))
    bins, me = lax.optimization_barrier((bins, me))
    own = unfold(exchange(bins).reshape(NFREQ, J, 8, 128))
    own, late_kernel = lax.optimization_barrier((own, kernel))

    across = shift(own, 0, 1)
    up = shift(own, 1, 0)
    down = shift(own, -1, 0)
    held, kept = hold(pltpu.with_memory_space_constraint(late_kernel, pltpu.HBM))
    across_down = shift(across, -1, 0)
    across_up = shift(across, 1, 0)
    far = shift(up, 1, 0)
    across_far = shift(across_down, -1, 0)
    blocks = [own, up, down, far, across, across_up, across_down, across_far]
    waves = exchange(forward(me, blocks, held))

    upgoing, back = truncate(waves.reshape(NFREQ * J * 8, SOURCES), table, onset_up)
    back = exchange(back.reshape(NFREQ, J, 8, SOURCES))

    (far, across_up, across_down, across_far), held = adjoint_remote(me, back, kernel, kept)
    own, up, down, across = adjoint_near(me, back, held)
    r1 = shift(across_far, 1, 0)
    r5 = shift(far, -1, 0)
    r3 = shift(across_up, -1, 0)
    r2 = shift(add(across_down, r1), 1, 0)
    r6 = shift(add(up, r5), -1, 0)
    r4 = shift(add(across, r2, r3), 0, 1)
    r7 = shift(down, 1, 0)
    summed = exchange(fold([own, r6, r7, r4]))

    updated = update(
        summed.reshape(NFREQ * J * 8, 2 * RECV),
        table,
        direct.reshape(2, UP_POINTS, RECV, NT),
        onset_back,
    )
    return (
        upgoing.reshape(UP_POINTS, SOURCES, NT),
        updated.reshape(POINTS, RECV, NT),
    )


def solution(mesh):
    placed = (
        P("src", "freq", None),
        P("src", "freq", None),
        P(None, "freq", "src", None),
        P("freq", "src"),
        P("src", "freq"),
    )
    return jax.shard_map(
        whole,
        mesh=mesh,
        in_specs=placed,
        out_specs=(P("freq", "src", None), P("src", "freq", None)),
        check_vma=False,
    )
```

```python
import functools
import math

import jax
import jax.numpy as jnp
from jax import lax
from jax.experimental import pallas as pl
from jax.experimental.pallas import tpu as pltpu
from jax.sharding import PartitionSpec as P


NT = 2048
NF = 192
BIN0 = 16
NFREQ = 16
NSRC = 8
NY = 4
J = NF // NFREQ
BANDS = 2
J2 = J // BANDS
ROWS = 2 * NF // BANDS
WIDE = 4 * ROWS
PART = WIDE // NFREQ
HT = NT // 2
POINTS = 8
UP_POINTS = 4
RECV = 64
R = NFREQ * RECV
SOURCES = 256
SCALE = 2.0 / NT
F32 = jnp.float32
BF16 = jnp.bfloat16


NT_DIMS = (((1,), (1,)), ((), ()))
TN_DIMS = (((0,), (0,)), ((), ()))

OWN, UP, DOWN, FAR, ACROSS, ACROSS_UP, ACROSS_DOWN, ACROSS_FAR = range(8)
RELATIVE = ((0, 0), (3, 0), (1, 0), (2, 0), (0, 1), (3, 1), (1, 1), (2, 1))
NEAR = (OWN, UP, DOWN, ACROSS)
REMOTE = (FAR, ACROSS_UP, ACROSS_DOWN, ACROSS_FAR)


LIMIT = 24 << 20
VMEM_SPEC = pl.BlockSpec(memory_space=pltpu.VMEM)
SMEM_SPEC = pl.BlockSpec(memory_space=pltpu.SMEM)
HBM_SPEC = pl.BlockSpec(memory_space=pltpu.HBM)


def cost(flops, bytes_accessed):
    return pl.CostEstimate(flops=flops, bytes_accessed=bytes_accessed, transcendentals=0)


def turn(phase):
    quarter = (phase + NT // 8) >> 9
    rest = (phase - (quarter << 9)).astype(F32) * (2.0 * math.pi / NT)
    square = rest * rest
    sine = rest * (
        1.0 + square * (-1.0 / 6 + square * (1.0 / 120 + square * (-1.0 / 5040 + square / 362880)))
    )
    cosine = 1.0 + square * (
        -0.5 + square * (1.0 / 24 + square * (-1.0 / 720 + square * (1.0 / 40320 - square / 3628800)))
    )
    odd = (quarter & 1) == 1
    first, second = jnp.where(odd, sine, cosine), jnp.where(odd, cosine, sine)
    behind = ((quarter + 1) & 2) == 2
    below = (quarter & 2) == 2
    return jnp.where(behind, -first, first), jnp.where(below, -second, second)


def write_table(table):
    lane = lax.broadcasted_iota(jnp.int32, (ROWS, 128), 1)
    row = lax.broadcasted_iota(jnp.int32, (ROWS, 128), 0)
    quarter = row & 1
    for parity in range(BANDS):
        bin_index = BIN0 + parity + row - quarter
        fine_cos, fine_sin = turn((lane * bin_index) & (NT - 1))
        coarse_cos, coarse_sin = turn(((lane * bin_index + 4 * quarter) & 15) << 7)
        for a in range(HT // 128):
            value = coarse_cos[:, a : a + 1] * fine_cos - coarse_sin[:, a : a + 1] * fine_sin
            table[parity, :, a * 128 : (a + 1) * 128] = value.astype(BF16)


def forward_bands(table, early, late):
    for parity, mixed in enumerate((early + late, early - late)):
        yield parity, lax.dot_general(
            table[parity], mixed.astype(BF16), NT_DIMS, preferred_element_type=F32
        )


def inverse_bands(table, bands):
    even, odd = [
        lax.dot_general(bands[p], table[p], TN_DIMS, preferred_element_type=F32)
        for p in range(BANDS)
    ]
    return (even + odd) * SCALE, (even - odd) * SCALE


def spectrum_body(traces, table, out, rows, wide, sems):
    copies = [
        pltpu.make_async_copy(traces.at[:, p], rows.at[p], sems.at[p]) for p in range(UP_POINTS)
    ]
    for copy in copies:
        copy.start()
    write_table(table)
    for p, copy in enumerate(copies):
        copy.wait()
        early = rows[p, :, :, :HT].reshape(2 * RECV, HT).astype(F32)
        late = rows[p, :, :, HT:].reshape(2 * RECV, HT).astype(F32)
        for parity, bins in forward_bands(table, early, late):
            wide.at[parity][pl.ds(p, ROWS, stride=UP_POINTS), :] = bins
    for parity in range(BANDS):
        for f in range(NFREQ):
            out[f, parity] = wide[parity, f * PART : f * PART + PART].astype(BF16)


def spectrum(traces):
    return pl.pallas_call(
        spectrum_body,
        in_specs=[HBM_SPEC],
        out_specs=[VMEM_SPEC] * 2,
        out_shape=[
            jax.ShapeDtypeStruct((BANDS, ROWS, HT), BF16),
            jax.ShapeDtypeStruct((NFREQ, BANDS, PART, 128), BF16),
        ],
        scratch_shapes=[
            pltpu.VMEM((UP_POINTS, 2, RECV, NT), BF16),
            pltpu.VMEM((BANDS, WIDE, 128), F32),
            pltpu.SemaphoreType.DMA((UP_POINTS,)),
        ],
        compiler_params=pltpu.CompilerParams(vmem_limit_bytes=LIMIT),
        cost_estimate=cost(POINTS * RECV * NT * 2 * ROWS, 4 << 20),
        name="spectrum",
    )(traces)


def unfold_body(bins, out):
    low = lax.broadcasted_iota(jnp.int32, (8, 128), 1) < RECV

    def step(j, carry):
        for pair in range(NFREQ // 2):
            even = bins[2 * pair, j].astype(F32)
            odd = bins[2 * pair + 1, j].astype(F32)
            first = jnp.where(low, even, pltpu.roll(odd, RECV, 1))
            second = jnp.where(low, pltpu.roll(even, RECV, 1), odd)
            both = jnp.concatenate([first, second], axis=0).astype(BF16)
            out[j, :, pair * 128 : pair * 128 + 128] = both
        return carry

    lax.fori_loop(0, J, step, 0, unroll=2)


def unfold(bins):
    return pl.pallas_call(
        unfold_body,
        in_specs=[VMEM_SPEC],
        out_specs=VMEM_SPEC,
        out_shape=jax.ShapeDtypeStruct((J, 2 * POINTS, R), BF16),
        compiler_params=pltpu.CompilerParams(vmem_limit_bytes=8 << 20),
        cost_estimate=cost(0, 1 << 20),
        name="unfold",
    )(bins)


def swapped(value, sign):
    rows, lanes = value.shape
    tiles = value.reshape(rows // 8, 2, 4, lanes)
    return jnp.concatenate([-sign * tiles[:, 1:], sign * tiles[:, :1]], axis=1).reshape(rows, lanes)


def places(me):
    y, z = me // 2, me % 2
    return [2 * ((y + dy) % NY) + (z + dz) % 2 for dy, dz in RELATIVE]


KEPT = 2


def hold_body(kern, held, kept, sems):
    copies = [
        pltpu.make_async_copy(kern.at[part], held.at[part], sems.at[part]) for part in range(2)
    ] + [
        pltpu.make_async_copy(kern.at[part, :KEPT], kept.at[part], sems.at[2 + part])
        for part in range(2)
    ]
    for copy in copies:
        copy.start()
    for copy in copies:
        copy.wait()


def hold(kern):
    return pl.pallas_call(
        hold_body,
        in_specs=[HBM_SPEC],
        out_specs=[pl.BlockSpec(memory_space=pl.ANY)] * 2,
        out_shape=[
            pltpu.VMEM(kern.shape, BF16),
            pltpu.VMEM((2, KEPT) + kern.shape[2:], BF16),
        ],
        scratch_shapes=[pltpu.SemaphoreType.DMA((4,))],
        compiler_params=pltpu.CompilerParams(vmem_limit_bytes=1 << 20),
        cost_estimate=cost(0, 13 << 20),
        name="hold",
    )(kern)


def forward_body(me, *refs):
    *blocks, kern, out = refs
    place = places(me[0])

    def step(j2, carry):
        for parity in range(BANDS):
            j = parity * J2 + j2
            at = BANDS * j2 + parity
            field = jnp.concatenate([b[j] for b in blocks], axis=0).T
            by_real = jnp.dot(kern[0, at], field, preferred_element_type=F32).T
            by_imag = jnp.dot(kern[1, at], field, preferred_element_type=F32).T
            waves = (by_real + swapped(by_imag, 1.0)).astype(BF16).reshape(NSRC, 2, 8, SOURCES)
            for rel in range(NSRC):
                for half in range(2):
                    out[2 * place[rel] + half, j] = waves[rel, half]
        return carry

    lax.fori_loop(0, J2, step, 0)


def forward(me, blocks, kern):
    return pl.pallas_call(
        forward_body,
        in_specs=[SMEM_SPEC] + [VMEM_SPEC] * (NSRC + 1),
        out_specs=VMEM_SPEC,
        out_shape=jax.ShapeDtypeStruct((NFREQ, J, 8, SOURCES), BF16),
        compiler_params=pltpu.CompilerParams(vmem_limit_bytes=8 << 20),
        cost_estimate=cost(8 * J * 64 * SOURCES * R, 4 << 20),
        name="forward",
    )(me, *blocks, kern)


PARTED = (ACROSS, ACROSS_DOWN, ACROSS_FAR)


def term_shapes(which):
    return [
        jax.ShapeDtypeStruct((J2 if rel in PARTED else J, 2 * POINTS, R), BF16)
        for rel in which
        for _ in range(BANDS if rel in PARTED else 1)
    ]


def terms_of(place, field_ref, held, which, outs, j2, parity):
    j = parity * J2 + j2
    at = BANDS * j2 + parity
    field = jnp.concatenate(
        [field_ref[2 * place[rel] + half, j] for rel in which for half in range(2)], axis=0
    )
    by_real = jnp.dot(field, held[0, at], preferred_element_type=F32)
    by_imag = jnp.dot(field, held[1, at], preferred_element_type=F32)
    terms = (by_real + swapped(by_imag, -1.0)).astype(BF16)
    position = 0
    for index, rel in enumerate(which):
        value = terms[index * 16 : index * 16 + 16]
        if rel in PARTED:
            outs[position + parity][j2] = value
            position += BANDS
        else:
            outs[position][j] = value
            position += 1


def adjoint_remote_body(me, field_ref, kern, kept, *refs):
    *outs, held, sems = refs
    place = places(me[0])

    def copies(at):
        return [
            pltpu.make_async_copy(kern.at[part, at], held.at[part, at], sems.at[part, at])
            for part in range(2)
        ]

    for at in range(J):
        for part in range(2):
            source = kept if at < KEPT else kern
            pltpu.make_async_copy(
                source.at[part, at], held.at[part, at], sems.at[part, at]
            ).start()

    def step(j2, carry):
        for parity in range(BANDS):
            for copy in copies(BANDS * j2 + parity):
                copy.wait()
            terms_of(place, field_ref, held, REMOTE, outs, j2, parity)
        return carry

    lax.fori_loop(0, J2, step, 0)


def adjoint_remote(me, field, kern, kept):
    shapes = term_shapes(REMOTE)
    *terms, held = pl.pallas_call(
        adjoint_remote_body,
        in_specs=[SMEM_SPEC, VMEM_SPEC, HBM_SPEC, VMEM_SPEC],
        out_specs=[VMEM_SPEC] * (len(shapes) + 1),
        out_shape=shapes + [pltpu.VMEM(kern.shape, BF16)],
        scratch_shapes=[pltpu.SemaphoreType.DMA((2, J))],
        compiler_params=pltpu.CompilerParams(vmem_limit_bytes=8 << 20),
        cost_estimate=cost(4 * J * 64 * SOURCES * R, 14 << 20),
        name="adjoint_remote",
    )(me, field, kern, kept)
    return terms, held


def adjoint_near_body(me, field_ref, held, *outs):
    place = places(me[0])

    def step(j2, carry):
        for parity in range(BANDS):
            terms_of(place, field_ref, held, NEAR, outs, j2, parity)
        return carry

    lax.fori_loop(0, J2, step, 0)


def adjoint_near(me, field, held):
    shapes = term_shapes(NEAR)
    return pl.pallas_call(
        adjoint_near_body,
        in_specs=[SMEM_SPEC, VMEM_SPEC, VMEM_SPEC],
        out_specs=[VMEM_SPEC] * len(shapes),
        out_shape=shapes,
        compiler_params=pltpu.CompilerParams(vmem_limit_bytes=8 << 20),
        cost_estimate=cost(4 * J * 64 * SOURCES * R, 2 << 20),
        name="adjoint_near",
    )(me, field, held)


def combine_body(first, second, third, out, *, start):
    def step(j, carry):
        total = first[j].astype(F32) + second[j].astype(F32) + third[start + j].astype(F32)
        out[j] = total.astype(BF16)
        return carry

    lax.fori_loop(0, J2, step, 0, unroll=2)


def combine(parity, first, second, third):
    return pl.pallas_call(
        functools.partial(combine_body, start=parity * J2),
        in_specs=[VMEM_SPEC] * 3,
        out_specs=VMEM_SPEC,
        out_shape=jax.ShapeDtypeStruct((J2, 2 * POINTS, R), BF16),
        compiler_params=pltpu.CompilerParams(vmem_limit_bytes=8 << 20),
        cost_estimate=cost(0, 1 << 20),
        name="combine",
    )(first, second, third)


def fold_body(*refs):
    *terms, even_part, odd_part, out = refs
    low = lax.broadcasted_iota(jnp.int32, (8, 128), 1) < RECV

    def step(j2, carry):
        for parity, part in enumerate((even_part, odd_part)):
            j = parity * J2 + j2
            total = part[j2].astype(F32)
            for term in terms:
                total = total + term[j].astype(F32)
            for pair in range(NFREQ // 2):
                first = total[:8, pair * 128 : pair * 128 + 128]
                second = total[8:, pair * 128 : pair * 128 + 128]
                out[2 * pair, j] = jnp.where(low, first, pltpu.roll(second, RECV, 1)).astype(BF16)
                out[2 * pair + 1, j] = jnp.where(low, pltpu.roll(first, RECV, 1), second).astype(BF16)
        return carry

    lax.fori_loop(0, J2, step, 0)


def fold(terms):
    return pl.pallas_call(
        fold_body,
        in_specs=[VMEM_SPEC] * len(terms),
        out_specs=VMEM_SPEC,
        out_shape=jax.ShapeDtypeStruct((NFREQ, J, 8, 128), BF16),
        compiler_params=pltpu.CompilerParams(vmem_limit_bytes=8 << 20),
        cost_estimate=cost(0, 2 << 20),
        name="fold",
    )(*terms)


PER = 2
LANES = [slice(half * 128, half * 128 + 128) for half in range(SOURCES // 128)]


def parts():
    for parity in range(BANDS):
        for f in range(NFREQ):
            start = (f * BANDS + parity) * PART
            yield parity, slice(f * PART, f * PART + PART), slice(start, start + PART)


def truncate_body(waves, table, onset, up, back, wide_in, wide_out, rows, sems):
    for parity, inner, outer in parts():
        for half, lanes in enumerate(LANES):
            wide_in[parity, half, inner] = waves[outer, lanes].astype(F32)
    sample = lax.broadcasted_iota(jnp.int32, (PER * SOURCES, HT), 1)
    copies = []
    for group in range(UP_POINTS // PER):
        points = [PER * group + index for index in range(PER)]
        every = [pl.ds(point, ROWS, stride=UP_POINTS) for point in points]
        bands = [
            jnp.concatenate(
                [wide_in.at[parity, half][e, :] for e in every for half in range(len(LANES))], axis=1
            ).astype(BF16)
            for parity in range(BANDS)
        ]
        limit = [
            jnp.broadcast_to(onset[p : p + 1, :].astype(F32), (128, SOURCES)).T[:, :1] for p in points
        ]
        limit = jnp.concatenate(limit, axis=0).astype(jnp.int32)
        kept = []
        for half, signal in enumerate(inverse_bands(table, bands)):
            kept.append(jnp.where(sample < limit - half * HT, signal, 0.0).astype(BF16))
            rows[group, :, half * HT : half * HT + HT] = kept[-1]
        span = pl.ds(group * PER * SOURCES, PER * SOURCES)
        copies.append(pltpu.make_async_copy(rows.at[group], up.at[span], sems.at[group]))
        copies[-1].start()
        for parity, bins in forward_bands(table, kept[0].astype(F32), kept[1].astype(F32)):
            for index, e in enumerate(every):
                for half in range(len(LANES)):
                    start = index * SOURCES + half * 128
                    wide_out.at[parity, half][e, :] = bins[:, start : start + 128]
    for parity, inner, outer in parts():
        for half, lanes in enumerate(LANES):
            back[outer, lanes] = wide_out[parity, half, inner].astype(BF16)
    for copy in copies:
        copy.wait()


def truncate(waves, table, onset):
    groups = UP_POINTS // PER
    return pl.pallas_call(
        truncate_body,
        in_specs=[VMEM_SPEC] * 3,
        out_specs=[pl.BlockSpec(memory_space=pl.ANY), VMEM_SPEC],
        out_shape=[
            pltpu.HBM((UP_POINTS * SOURCES, NT), BF16),
            jax.ShapeDtypeStruct(waves.shape, BF16),
        ],
        scratch_shapes=[pltpu.VMEM((BANDS, len(LANES), WIDE, 128), F32)] * 2
        + [
            pltpu.VMEM((groups, PER * SOURCES, NT), BF16),
            pltpu.SemaphoreType.DMA((groups,)),
        ],
        compiler_params=pltpu.CompilerParams(vmem_limit_bytes=40 << 20),
        cost_estimate=cost(2 * UP_POINTS * SOURCES * NT * 2 * ROWS, 8 << 20),
        name="truncate",
    )(waves, table, onset)


def update_body(bins, table, direct, onset, out, wide, rows, sems):
    for parity, inner, outer in parts():
        wide[parity, inner] = bins[outer, :].astype(F32)
    sample = lax.broadcasted_iota(jnp.int32, (2 * RECV, HT), 1)
    copies = []
    for p in range(UP_POINTS):
        every = pl.ds(p, ROWS, stride=UP_POINTS)
        bands = [wide.at[parity][every, :].astype(BF16) for parity in range(BANDS)]
        row = jnp.concatenate([onset[p : p + 1, :], onset[p + 4 : p + 5, :]], axis=1).astype(F32)
        limit = jnp.broadcast_to(row, (128, 2 * RECV)).T[:, :1].astype(jnp.int32)
        for half, trace in enumerate(inverse_bands(table, bands)):
            span = slice(half * HT, half * HT + HT)
            cut = jnp.where(sample < limit - half * HT, trace, 0.0)
            before = direct[:, p, :, span].reshape(2 * RECV, HT).astype(F32)
            rows[p, :, :, span] = (before - cut).astype(BF16).reshape(2, RECV, HT)
        copies.append(pltpu.make_async_copy(rows.at[p], out.at[:, p], sems.at[p]))
        copies[-1].start()
    for copy in copies:
        copy.wait()


def update(bins, table, direct, onset):
    return pl.pallas_call(
        update_body,
        in_specs=[VMEM_SPEC] * 4,
        out_specs=pl.BlockSpec(memory_space=pl.ANY),
        out_shape=pltpu.HBM((2, UP_POINTS, RECV, NT), BF16),
        scratch_shapes=[
            pltpu.VMEM((BANDS, WIDE, 2 * RECV), F32),
            pltpu.VMEM((UP_POINTS, 2, RECV, NT), BF16),
            pltpu.SemaphoreType.DMA((UP_POINTS,)),
        ],
        compiler_params=pltpu.CompilerParams(vmem_limit_bytes=LIMIT),
        cost_estimate=cost(POINTS * RECV * NT * 2 * ROWS, 5 << 20),
        name="update",
    )(bins, table, direct, onset)


def shift(value, dy, dz):
    pairs = [
        (2 * y + z, 2 * ((y + dy) % NY) + (z + dz) % 2) for y in range(NY) for z in range(2)
    ]
    return lax.ppermute(value, "src", pairs)


def add(*terms):
    return functools.reduce(lambda a, b: a + b, [t.astype(F32) for t in terms]).astype(BF16)


def exchange(value):
    return lax.all_to_all(value, "freq", split_axis=0, concat_axis=0, tiled=True)


def whole(focusing, direct, kernel, onset_up, onset_back):
    me = lax.axis_index("src").reshape(1)
    kernel = pltpu.with_memory_space_constraint(kernel, pltpu.HBM)

    traces = focusing.reshape(2, UP_POINTS, RECV, NT)
    table, bins = spectrum(pltpu.with_memory_space_constraint(traces, pltpu.HBM))
    bins, me = lax.optimization_barrier((bins, me))
    own = unfold(exchange(bins).reshape(NFREQ, J, 8, 128))
    own, late_kernel = lax.optimization_barrier((own, kernel))

    across = shift(own, 0, 1)
    up = shift(own, 1, 0)
    down = shift(own, -1, 0)
    held, kept = hold(pltpu.with_memory_space_constraint(late_kernel, pltpu.HBM))
    across_down = shift(across, -1, 0)
    across_up = shift(across, 1, 0)
    far = shift(up, 1, 0)
    across_far = shift(across_down, -1, 0)
    blocks = [own, up, down, far, across, across_up, across_down, across_far]
    waves = exchange(forward(me, blocks, held))

    upgoing, back = truncate(waves.reshape(NFREQ * J * 8, SOURCES), table, onset_up)
    back = exchange(back.reshape(NFREQ, J, 8, SOURCES))

    terms, held = adjoint_remote(me, back, kernel, kept)
    far, across_up, *parted = terms
    across_down, across_far = parted[:BANDS], parted[BANDS:]
    own, up, down, *across = adjoint_near(me, back, held)
    r3 = shift(across_up, -1, 0)
    r5 = shift(far, -1, 0)
    last = []
    for parity in range(BANDS):
        r1 = shift(across_far[parity], 1, 0)
        r2 = shift(add(across_down[parity], r1), 1, 0)
        both = combine(parity, across[parity], r2, r3)
        last.append(shift(both, 0, 1))
    r6 = shift(add(up, r5), -1, 0)
    r7 = shift(down, 1, 0)
    summed = exchange(fold([own, r6, r7, *last]))

    updated = update(
        summed.reshape(NFREQ * J * 8, 2 * RECV),
        table,
        direct.reshape(2, UP_POINTS, RECV, NT),
        onset_back,
    )
    return (
        upgoing.reshape(UP_POINTS, SOURCES, NT),
        updated.reshape(POINTS, RECV, NT),
    )


def solution(mesh):
    placed = (
        P("src", "freq", None),
        P("src", "freq", None),
        P(None, "freq", "src", None),
        P("freq", "src"),
        P("src", "freq"),
    )
    return jax.shard_map(
        whole,
        mesh=mesh,
        in_specs=placed,
        out_specs=(P("freq", "src", None), P("src", "freq", None)),
        check_vma=False,
    )
```
